32 devices in a mesh: groups: 2 (over x), ta: 16 (over z, y, core).
Axes of the slice: x: 2, y: 2, z: 4, core: 2. Of those that a mesh axis runs over, the one named last changes fastest.
Arguments:
- source: float32 [32, 4, 32, 256], P(('groups', 'ta')), parts along dimension 0, may hold values from -13 to 13
- links: float32 [16, 4, 9, 256, 256], P('ta'), may hold values from -0.046875 to 0.046875
- prolongator: float32 [16, 4, 16, 256], P('ta'), may hold values from -0.375 to 0.375
- coarse_inverse: float32 [1024, 1024], P('ta'), may hold values from -1 to 2
Outputs:
- solution: float32 [32, 4, 32, 256], P(('groups', 'ta')), parts along dimension 0
- residual: float32 [32, 4, 32, 256], P(('groups', 'ta')), parts along dimension 0
The draws below stay inside these ranges and needn't reach their ends.
There are 2 independent parts, one for each index of `groups`. The reference program is written for one: setup_inputs(seed, part) draws one part's arguments, and reference() takes and returns one part's arrays. A program takes and returns all parts, laid end to end along the dimension named above; an argument that names none is the same for every part. Nothing has to cross between parts.
All inputs are finite; a program needn't handle non-finite values.
Results may differ from the reference program's by a relative error of at most 0.0003.
Values sent between devices are 32-bit elements; how exact they have to be, the bound alone decides.
A program may use at most 64 MiB of HBM per device.

```python
import jax
import jax.numpy as jnp
from jax import lax

NC = 256
RHS = 32
LX = 1
LY = 2
LZ = 2
SWEEPS = 3
NT = 16
SP = 4
KS = 16
NCOARSE = 1024


def draw_source(key, part):
    noise_key = jax.random.fold_in(key, 11)
    noise = jnp.clip(jax.random.normal(noise_key, (NT, SP, RHS, NC), jnp.float32), -4.0, 4.0)
    ramped = 0.5 + jnp.arange(NT, dtype=jnp.float32) / max(NT - 1, 1)
    return noise * ramped[:, None, None, None]


def draw_coarse_inverse(key, part):
    noise_key = jax.random.fold_in(key, 21)
    spread = jnp.clip(jax.random.normal(noise_key, (NCOARSE, NCOARSE), jnp.float32), -4.0, 4.0)
    diagonal = jnp.ones((NCOARSE,), jnp.float32)
    return spread * NCOARSE ** (-0.5) + jnp.diag(diagonal)


def shard_levels(own_key, shape, pieces, low, largest):
    level = 1.0
    for axis_at, blocks in pieces:
        steps = jax.random.uniform(jax.random.fold_in(jax.random.fold_in(own_key, 6), axis_at), (blocks,), jnp.float32, low / len(pieces), largest / len(pieces))
        level = level * jnp.repeat(jnp.exp(steps), shape[axis_at] // blocks).reshape((-1,) + (1,) * (len(shape) - 1 - axis_at))
    return level


def bell_draw(own_key, extent, deviation, limit, pieces=(), held_as=jnp.bfloat16):
    loudness = shard_levels(own_key, extent, pieces, -0.22, 0.18) if pieces else 1.0
    entries = jax.random.normal(own_key, extent, jnp.float32) * deviation * loudness
    return jnp.minimum(jnp.maximum(entries, -limit), limit).astype(held_as)


def setup_inputs(seed: int = 0, part: int = 0) -> dict:
    splits = jax.random.split(jax.random.key(seed), 5)
    own_keys = jax.random.split(jax.random.fold_in(splits[4], part), 5)
    source = draw_source(jax.random.fold_in(jax.random.fold_in(splits[4], part), 71), part)
    links = bell_draw(splits[1], (NT, SP, 9, NC, NC), (0.12 * NC ** -0.5), 0.046875, ((0, 16),), jnp.float32)
    prolongator = bell_draw(splits[2], (NT, SP, KS, NC), NC ** -0.5, 0.375, ((0, 16),), jnp.float32)
    coarse_inverse = draw_coarse_inverse(jax.random.fold_in(splits[4], 71), part)
    return dict(source=source, links=links, prolongator=prolongator, coarse_inverse=coarse_inverse)


damping = 0.8
full_precision = lax.Precision.HIGHEST


def neighbours(field):
    grid = field.reshape(NT, LX, LY, LZ, RHS, NC)

    def rolled(amount, axis):
        return jnp.roll(grid, amount, axis).reshape(field.shape)

    return jnp.stack([field, rolled(-1, 0), rolled(1, 0), rolled(-1, 1), rolled(1, 1),
                      rolled(-1, 2), rolled(1, 2), rolled(-1, 3), rolled(1, 3)], axis=2)


def operate(links, field):
    return field + jnp.einsum("tsmab,tsmjb->tsja", links, neighbours(field),
                              precision=full_precision, preferred_element_type=jnp.float32)


def inner(first, second):
    return jnp.sum(first * second, axis=(0, 1, 3))


def smooth(links, solution, residual):
    for sweep in range(SWEEPS):
        image = operate(links, residual)
        factor = (damping * inner(image, residual) / inner(image, image))[:, None]
        solution = solution + factor * residual
        residual = residual - factor * image
    return solution, residual


def reference(source, links, prolongator, coarse_inverse):
    solution = jnp.zeros_like(source)
    residual = source
    solution, residual = smooth(links, solution, residual)
    restricted = jnp.einsum("tskc,tsjc->tskj", prolongator, residual,
                            precision=full_precision, preferred_element_type=jnp.float32).reshape(NCOARSE, RHS)
    coarse = jnp.dot(coarse_inverse, restricted, precision=full_precision, preferred_element_type=jnp.float32)
    correction = jnp.einsum("tskc,tskj->tsjc", prolongator, coarse.reshape(NT, SP, KS, RHS),
                            precision=full_precision, preferred_element_type=jnp.float32)
    image = operate(links, correction)
    factor = (inner(image, residual) / inner(image, image))[:, None]
    solution = solution + factor * correction
    residual = residual - factor * image
    solution, residual = smooth(links, solution, residual)
    return solution, residual
```

```python
import functools

import jax
import jax.numpy as jnp
from jax import lax
from jax.experimental import pallas as pl
from jax.experimental.pallas import tpu as pltpu
from jax.sharding import PartitionSpec as P

LINK_SUMS = ((0, 3, 4), (5, 6), (7, 8), (1,), (2,))
INNER_SUMS = 3
DAMPING = 0.8
SWEEPS = 3
STEP = 0.8
HIGHEST = lax.Precision.HIGHEST
F32 = jnp.float32
BF16 = jnp.bfloat16
SMALL_ROWS = 2


def dot(a, b):
    return jnp.dot(a, b, precision=HIGHEST, preferred_element_type=F32)


def kernel(
    n,
    source_ref,
    links_ref,
    prol_ref,
    inverse_ref,
    solution_ref,
    residual_ref,
    source_in,
    prol_in,
    inverse_in,
    raw,
    lcat,
    weights,
    field,
    outgoing,
    halo,
    prol_halo,
    coarse_out,
    coarse_halo,
    acc,
    stage,
    gather,
    small_stage,
    small,
    rall,
    gcat,
    xcat,
    input_sem,
    link_sem,
    halo_send,
    halo_recv,
    near_send,
    near_recv,
    gather_send,
    gather_recv,
    small_send,
    small_recv,
):
    me = lax.axis_index("ta")
    sites, rhs, comps = source_ref.shape[1:]
    ks = prol_ref.shape[2]
    width = sites * rhs
    right, left = lax.rem(me + 1, n), lax.rem(me + n - 1, n)

    barrier = pltpu.get_barrier_semaphore()

    def greet(d, carry):
        pl.semaphore_signal(barrier, inc=1, device_id={"ta": lax.rem(me + d, n)})
        return carry

    lax.fori_loop(1, n, greet, 0)
    inputs = [
        pltpu.make_async_copy(hbm, vmem, input_sem.at[i])
        for i, (hbm, vmem) in enumerate(
            ((source_ref, source_in), (prol_ref, prol_in), (inverse_ref, inverse_in))
        )
    ]
    inputs[0].start()
    inputs[1].start()
    for s in range(sites):
        pltpu.make_async_copy(links_ref.at[0, s], raw.at[s], link_sem.at[s]).start()
    inputs[2].start()

    lane_site = lax.broadcasted_iota(jnp.int32, (1, width), 1) // rhs
    even = lane_site % 2 == 0

    def over_sites(x):
        shift = rhs
        while shift < width:
            x = x + pltpu.roll(x, shift, 1)
            shift *= 2
        return x

    row_site = lax.broadcasted_iota(jnp.int32, (sites * ks, width), 0) // ks
    diagonal = row_site == lax.broadcasted_iota(jnp.int32, (sites * ks, width), 1) // rhs

    def two_parts(a):
        hi = a.astype(BF16)
        return hi, (a - hi.astype(F32)).astype(BF16)


    def dot_parts(a, b):
        p = jnp.dot(a, b, preferred_element_type=F32)
        rows = a.shape[0] // 2
        return p[:rows, :width] + p[:rows, width:] + p[rows:, :width]

    def restrict():
        full = jnp.where(diagonal, dot_parts(prol_parts, weights[:comps]), 0.0)
        return functools.reduce(jnp.add, [full[s * ks : (s + 1) * ks] for s in range(sites)])

    def products(pairs, rows=1):
        packed = []
        for at in range(0, rows * sites, sites):
            row = jnp.zeros((1, width), F32)
            for i, (a, b) in enumerate(pairs[at : at + sites]):
                row = jnp.where(lane_site == i, over_sites(jnp.sum(a * b, axis=0, keepdims=True)), row)
            packed.append(row)
        return packed[0] if rows == 1 else jnp.concatenate(packed, axis=0)

    block = comps // sites

    def send_site(r, s, v):
        message = jnp.zeros((block, width), F32)
        for q in range(sites):
            moved = pltpu.roll(
                v[q * block : (q + 1) * block], lax.rem(q + sites - s, sites) * rhs, 1
            )
            message = jnp.where(lane_site == q, moved, message)
        outgoing[r, s] = message
        for side, to in ((0, left), (1, right)):
            pltpu.make_async_remote_copy(
                src_ref=outgoing.at[r, s],
                dst_ref=halo.at[r, side, s],
                send_sem=halo_send.at[r, side],
                recv_sem=halo_recv.at[r, side, s],
                device_id={"ta": to},
            ).start()

    def send_field(r, f):
        def one(s, carry):
            send_site(r, s, field[f])
            return carry

        lax.fori_loop(0, sites, one, 0)

    def near(k, src, dst):
        return [
            pltpu.make_async_remote_copy(
                src_ref=src,
                dst_ref=dst.at[side],
                send_sem=near_send.at[k, side],
                recv_sem=near_recv.at[k, side],
                device_id={"ta": to},
            )
            for side, to in ((0, left), (1, right))
        ]

    def exchange(k, value, staged, slots, send_sem, recv_sem):
        staged[k] = value
        slots[k, me] = value

        def one(d, carry):
            pltpu.make_async_remote_copy(
                src_ref=staged.at[k],
                dst_ref=slots.at[k, me],
                send_sem=send_sem.at[k],
                recv_sem=recv_sem.at[k],
                device_id={"ta": lax.rem(me + d, n)},
            ).start()
            return carry

        lax.fori_loop(1, n, one, 0)
        return pltpu.make_async_remote_copy(
            src_ref=slots.at[k, pl.ds(0, n - 1)],
            dst_ref=slots.at[k, pl.ds(0, n - 1)],
            send_sem=send_sem.at[k],
            recv_sem=recv_sem.at[k],
            device_id={"ta": right},
        )

    pending = []

    def exchange_large(k, value):
        c = exchange(k, value, stage, gather, gather_send, gather_recv)
        pending.append(c)
        return c

    def exchange_small(k, value):
        c = exchange(k, value, small_stage, small, small_send, small_recv)
        pending.append(c)
        return c

    def load_weights(at, v):
        hi = v.astype(BF16)
        lo = (v - hi.astype(F32)).astype(BF16)
        weights[at * comps : (at + 1) * comps, :width] = hi
        weights[at * comps : (at + 1) * comps, width:] = lo

    def product(s, lo_k, hi_k):
        k = slice(lo_k * comps, hi_k * comps)
        p = jnp.dot(lcat[s, :comps, k], weights[k], preferred_element_type=F32)
        q = jnp.dot(lcat[s, comps:, k], weights[k, :width], preferred_element_type=F32)
        return p[:, :width] + p[:, width:] + q

    def load_inner(f):
        v = field[f]
        load_weights(0, v)
        load_weights(1, pltpu.roll(v, width // 2, 1))
        load_weights(2, jnp.where(even, pltpu.roll(v, width - rhs, 1), pltpu.roll(v, rhs, 1)))

    def inner():
        def site(s, carry):
            acc[...] = jnp.where(lane_site == s, product(s, 0, INNER_SUMS), acc[...])
            return carry

        lax.fori_loop(0, sites, site, 0, unroll=True)

    def outer(r, f, to, of_field, of_links, send=None):
        def site(s, carry):
            if r is not None:
                for side in range(2):
                    pltpu.make_async_remote_copy(
                        src_ref=outgoing.at[r, s],
                        dst_ref=halo.at[r, side, s],
                        send_sem=halo_send.at[r, side],
                        recv_sem=halo_recv.at[r, side, s],
                        device_id={"ta": left},
                    ).wait_recv()
                    m = halo[r, side, s]
                    load_weights(
                        INNER_SUMS + side,
                        jnp.concatenate(
                            [
                                pltpu.roll(m, lax.rem(s + sites - q, sites) * rhs, 1)
                                for q in range(sites)
                            ],
                            axis=0,
                        ),
                    )
            new = of_field * field[f] + of_links * (acc[...] + product(s, INNER_SUMS, len(LINK_SUMS)))
            field[to] = jnp.where(lane_site == s, new, field[to])
            if send is not None:
                send_site(send, s, new)
            return carry

        lax.fori_loop(0, sites, site, 0)

    def image_of(c):
        last = len(c) - 1
        inside = [(c[i] - c[i - 1]) / STEP for i in range(1, last + 1)]
        return [c[0] / STEP] + inside + [-c[last] / STEP]

    def factor_of(gram, c, d):
        gd = [
            functools.reduce(jnp.add, [gram(i, j) * d[j] for j in range(len(d))])
            for i in range(len(d))
        ]
        across = functools.reduce(jnp.add, [gd[i] * c[i] for i in range(len(c))])
        squared = functools.reduce(jnp.add, [gd[i] * d[i] for i in range(len(d))])
        return DAMPING * across / squared

    def advance(c, x, d, factor):
        x = [x[i] + factor * c[i] if i < len(c) else x[i] for i in range(SWEEPS)]
        return [c[i] - factor * d[i] if i < len(c) else -factor * d[i] for i in range(len(d))], x

    def sweeps(gram, count):
        c = [jnp.ones((1, width), F32)]
        x = [jnp.zeros((1, width), F32)] * SWEEPS
        for _ in range(count):
            d = image_of(c)
            c, x = advance(c, x, d, factor_of(gram, c, d))
        return c, x

    def combine(coefficients, fields):
        return functools.reduce(jnp.add, [a * field[f] for a, f in zip(coefficients, fields)])

    half = sites * ks
    inputs[0].wait()
    field[0] = source_in[0].reshape(width, comps).T
    pl.semaphore_wait(barrier, n - 1)
    send_field(0, 0)
    inputs[1].wait()
    prol_copies = near(0, prol_in.at[0], prol_halo)
    for copy in prol_copies:
        copy.start()
    prol = prol_in[0].reshape(half, comps)
    prol_parts = jnp.concatenate(two_parts(prol), axis=0)

    def prepare(s, carry):
        pltpu.make_async_copy(links_ref.at[0, s], raw.at[s], link_sem.at[s]).wait()
        for at, members in enumerate(LINK_SUMS):
            total = functools.reduce(jnp.add, [raw[s, m] for m in members])
            hi = total.astype(BF16)
            lo = (total - hi.astype(F32)).astype(BF16)
            lcat[s, :comps, at * comps : (at + 1) * comps] = hi
            lcat[s, comps:, at * comps : (at + 1) * comps] = lo
        return carry

    lax.fori_loop(0, sites, prepare, 0)
    for k in range(SWEEPS + 1):
        load_inner(k)
        value = jnp.concatenate(
            [restrict(), products([(field[k], field[i]) for i in range(k + 1)])], axis=0
        )
        exchange_large(k, value)
        if k == SWEEPS:
            send_field(k, k)
        inner()
        if k < SWEEPS:
            outer(k, k, k + 1, 1.0 - STEP, -STEP, k + 1 if k + 1 < SWEEPS else None)

    for copy in prol_copies:
        copy.wait_recv()

    def columns_of(p):
        hi = p.astype(BF16).astype(F32)
        return jnp.concatenate([hi, p - hi], axis=0).T.astype(BF16)

    bases = [columns_of(p.reshape(half, comps)) for p in (prol, prol_halo[0], prol_halo[1])]
    vectors = jnp.concatenate([prol, prol], axis=0).T
    g_lane = lax.broadcasted_iota(jnp.int32, (1, 2 * half), 1)
    g_site, g_low = lax.rem(g_lane, half) // ks, g_lane < half

    def operate_on_bases(s, carry):
        def times(m, base):
            k = slice(m * comps, (m + 1) * comps)
            r = jnp.dot(lcat[s, :comps, k], base, preferred_element_type=F32)
            r = r + jnp.dot(lcat[s, comps:, k], base, preferred_element_type=F32)
            return r + pltpu.roll(r, half, 1)

        across = s + 1 - 2 * lax.rem(s, 2)
        own = jnp.where(g_site == s, vectors + times(0, bases[0]), 0.0)
        own = jnp.where(g_site == lax.rem(s + sites // 2, sites), times(1, bases[0]), own)
        own = jnp.where(g_site == across, times(2, bases[0]), own)
        ahead = jnp.where(g_site == s, times(3, bases[1]), 0.0)
        behind = jnp.where((g_site == s) & g_low, times(4, bases[2]), 0.0)
        for at, value in enumerate((jnp.where(g_low, own, ahead), behind)):
            hi, lo = two_parts(value)
            lanes = slice(at * 2 * half, (at + 1) * 2 * half)
            gcat[s, :comps, lanes] = hi
            gcat[s, comps:, lanes] = lo
        return carry

    lax.fori_loop(0, sites, operate_on_bases, 0)
    inputs[2].wait()
    inverse_parts = jnp.concatenate(two_parts(inverse_in[...]), axis=0)

    def total_of(slots, k, at, rows):
        return jnp.sum(slots[k, :, at : at + rows, :], axis=0)

    def unpack(total, i):
        row = total[i // sites : i // sites + 1]
        return over_sites(jnp.where(lane_site == i % sites, row, 0.0))

    def solve_coarse(coefficients):
        def spread(t, carry):
            r = functools.reduce(
                jnp.add, [a * gather[k, t, :ks] for k, a in enumerate(coefficients)]
            )
            for s in range(sites):
                hi, lo = two_parts(jnp.where(lane_site == s, r, 0.0))
                at = pl.ds(pl.multiple_of((t * sites + s) * ks, ks), ks)
                rall[at, :width] = hi
                rall[at, width:] = lo
            return carry

        lax.fori_loop(0, n, spread, 0)
        return over_sites(dot_parts(inverse_parts, rall[...]))

    def store_coarse(at, x):
        hi, lo = two_parts(x)
        xcat[at * half : (at + 1) * half, :width] = hi
        xcat[at * half : (at + 1) * half, width:] = lo

    grams = {}

    def gram(i, j):
        return grams[max(i, j), min(i, j)]

    def read_grams(k):
        pending[k].wait_recv()
        total = total_of(gather, k, ks, 1)
        grams.update({(k, i): unpack(total, i) for i in range(k + 1)})

    for k in range(SWEEPS):
        read_grams(k)
    c, x = sweeps(gram, SWEEPS - 1)
    d = image_of(c)
    before = solve_coarse(c)
    xcat[3 * half :] = jnp.zeros((xcat.shape[0] - 3 * half, 2 * width), BF16)
    read_grams(SWEEPS)
    factor = factor_of(gram, c, d)
    coarse = before - factor * solve_coarse(d)
    compact = functools.reduce(
        jnp.add,
        [jnp.where(lane_site == s, coarse[s * ks : (s + 1) * ks], 0.0) for s in range(sites)],
    )
    coarse_out[...] = compact
    coarse_copies = near(1, coarse_out, coarse_halo)
    for copy in coarse_copies:
        copy.start()
    c, x = advance(c, x, d, factor)
    store_coarse(0, coarse)
    outer(SWEEPS, SWEEPS, SWEEPS + 1, 1.0 - STEP, -STEP)
    field[7] = combine(c, range(SWEEPS + 1))
    for side in range(2):
        coarse_copies[side].wait_recv()
        there = coarse_halo[side]
        store_coarse(
            1 + side,
            jnp.concatenate(
                [over_sites(jnp.where(lane_site == s, there, 0.0)) for s in range(sites)], axis=0
            ),
        )

    def operate_on_coarse(s, carry):
        p = jnp.dot(gcat[s, :comps], xcat[...], preferred_element_type=F32)
        q = jnp.dot(gcat[s, comps:], xcat[:, :width], preferred_element_type=F32)
        new = p[:, :width] + p[:, width:] + q
        field[6] = jnp.where(lane_site == s, new, field[6])
        send_site(4, s, new)
        return carry

    lax.fori_loop(0, sites, operate_on_coarse, 0)
    exchange_small(0, products([(field[6], field[7]), (field[6], field[6])], SMALL_ROWS))
    load_inner(6)
    inner()
    field[8] = combine(c, range(1, SWEEPS + 2))
    field[9] = combine(x, range(SWEEPS))
    field[5] = dot(prol.T, jnp.where(diagonal, coarse, 0.0))
    outer(4, 6, 14, 1.0 - STEP, -STEP)
    pending[-1].wait_recv()
    pair = total_of(small, 0, 0, SMALL_ROWS)
    g = unpack(pair, 0) / unpack(pair, 1)

    field[11] = field[8] - g * field[14]
    send_field(5, 11)
    field[10] = field[7] - g * field[6]
    field[9] = field[9] + g * field[5]
    load_inner(11)
    inner()
    outer(5, 11, 12, 1.0 - STEP, -STEP, 6)
    early = [(i, j) for i in range(3) for j in range(i + 1)]
    late = [(3, j) for j in range(4)]
    exchange_small(1, products([(field[10 + i], field[10 + j]) for i, j in early], SMALL_ROWS))
    load_inner(12)
    inner()
    outer(6, 12, 13, 1.0 - STEP, -STEP)
    exchange_small(2, products([(field[10 + i], field[10 + j]) for i, j in late], SMALL_ROWS))
    for r in range(halo.shape[0]):
        for side in range(2):
            pltpu.make_async_remote_copy(
                src_ref=outgoing.at[r],
                dst_ref=halo.at[r, side],
                send_sem=halo_send.at[r, side],
                recv_sem=halo_recv.at[r, side, 0],
                device_id={"ta": left},
            ).wait_send()
    for copy in pending[:-1] + prol_copies + coarse_copies:
        copy.wait_send()
    pending[-2].wait_recv()
    total = total_of(small, 1, 0, SMALL_ROWS)
    grams = {pair: unpack(total, early.index(pair)) for pair in early}
    c, x = sweeps(gram, SWEEPS - 1)
    d = image_of(c)
    pending[-1].wait_recv()
    total = total_of(small, 2, 0, SMALL_ROWS)
    grams.update({pair: unpack(total, late.index(pair)) for pair in late})
    c, x = advance(c, x, d, factor_of(gram, c, d))
    residual_ref[...] = combine(c, range(10, 14))
    solution_ref[...] = field[9] + combine(x, range(10, 13))
    pending[-1].wait_send()


def turn(*refs):
    for column, row in zip(refs[:2], refs[2:]):
        row[0] = column[...].T.reshape(row.shape[1:])


def local(source, links, prolongator, coarse_inverse):
    n = lax.axis_size("ta")
    _, sites, rhs, comps = source.shape
    ks = prolongator.shape[2]
    width = sites * rhs
    sums = len(LINK_SUMS)
    vmem = pl.BlockSpec(memory_space=pltpu.VMEM)
    dma = pltpu.SemaphoreType.DMA
    columns = pl.pallas_call(
        functools.partial(kernel, n),
        out_shape=(jax.ShapeDtypeStruct((comps, width), F32),) * 2,
        in_specs=[pl.BlockSpec(memory_space=pl.ANY)] * 4,
        out_specs=(vmem, vmem),
        scratch_shapes=[
            pltpu.VMEM(source.shape, F32),
            pltpu.VMEM(prolongator.shape, F32),
            pltpu.VMEM(coarse_inverse.shape, F32),
            pltpu.VMEM(links.shape[1:], F32),
            pltpu.VMEM((sites, 2 * comps, sums * comps), BF16),
            pltpu.VMEM((sums * comps, 2 * width), BF16),
            pltpu.VMEM((15, comps, width), F32),
            pltpu.VMEM((7, sites, comps // sites, width), F32),
            pltpu.VMEM((7, 2, sites, comps // sites, width), F32),
            pltpu.VMEM((2, *prolongator.shape[1:]), F32),
            pltpu.VMEM((ks, width), F32),
            pltpu.VMEM((2, ks, width), F32),
            pltpu.VMEM((comps, width), F32),
            pltpu.VMEM((SWEEPS + 1, ks + 1, width), F32),
            pltpu.VMEM((SWEEPS + 1, n, ks + 1, width), F32),
            pltpu.VMEM((3, SMALL_ROWS, width), F32),
            pltpu.VMEM((3, n, SMALL_ROWS, width), F32),
            pltpu.VMEM((n * sites * ks, 2 * width), BF16),
            pltpu.VMEM((sites, 2 * comps, 4 * sites * ks), BF16),
            pltpu.VMEM((4 * sites * ks, 2 * width), BF16),
            dma((3,)),
            dma((sites,)),
            dma((7, 2)),
            dma((7, 2, sites)),
            dma((2, 2)),
            dma((2, 2)),
            dma((SWEEPS + 1,)),
            dma((SWEEPS + 1,)),
            dma((3,)),
            dma((3,)),
        ],
        compiler_params=pltpu.CompilerParams(
            collective_id=0, has_side_effects=True, vmem_limit_bytes=60 * 1024 * 1024
        ),
    )(source, links, prolongator, coarse_inverse)
    return pl.pallas_call(
        turn,
        out_shape=(jax.ShapeDtypeStruct(source.shape, F32),) * 2,
        in_specs=[vmem, vmem],
        out_specs=(vmem, vmem),
    )(*columns)


def solution(mesh):
    return jax.shard_map(
        local,
        mesh=mesh,
        in_specs=(
            P(("groups", "ta"), None, None, None),
            P("ta", None, None, None, None),
            P("ta", None, None, None),
            P("ta", None),
        ),
        out_specs=(P(("groups", "ta"), None, None, None), P(("groups", "ta"), None, None, None)),
        check_vma=False,
    )
```

```python
import functools

import jax
import jax.numpy as jnp
from jax import lax
from jax.experimental import pallas as pl
from jax.experimental.pallas import tpu as pltpu
from jax.sharding import PartitionSpec as P

LINK_SUMS = ((0, 3, 4), (5, 6), (7, 8), (1,), (2,))
INNER_SUMS = 3
DAMPING = 0.8
SWEEPS = 3
STEP = 0.8
HIGHEST = lax.Precision.HIGHEST
F32 = jnp.float32
BF16 = jnp.bfloat16
SMALL_ROWS = 2


def dot(a, b):
    return jnp.dot(a, b, precision=HIGHEST, preferred_element_type=F32)


def kernel(
    n,
    source_ref,
    links_ref,
    prol_ref,
    inverse_ref,
    solution_ref,
    residual_ref,
    source_in,
    prol_in,
    inverse_in,
    raw,
    lcat,
    weights,
    field,
    outgoing,
    halo,
    prol_halo,
    coarse_out,
    coarse_halo,
    acc,
    stage,
    gather,
    small_stage,
    small,
    rall,
    gcat,
    xcat,
    input_sem,
    link_sem,
    halo_send,
    halo_recv,
    near_send,
    near_recv,
    gather_send,
    gather_recv,
    share_send,
    share_recv,
    small_send,
    small_recv,
):
    me = lax.axis_index("ta")
    sites, rhs, comps = source_ref.shape[1:]
    ks = prol_ref.shape[2]
    width = sites * rhs
    right, left = lax.rem(me + 1, n), lax.rem(me + n - 1, n)

    barrier = pltpu.get_barrier_semaphore()

    def greet(d, carry):
        pl.semaphore_signal(barrier, inc=1, device_id={"ta": lax.rem(me + d, n)})
        return carry

    lax.fori_loop(1, n, greet, 0)
    inputs = [
        pltpu.make_async_copy(hbm, vmem, input_sem.at[i])
        for i, (hbm, vmem) in enumerate(
            ((source_ref, source_in), (prol_ref, prol_in), (inverse_ref, inverse_in))
        )
    ]
    inputs[0].start()
    inputs[1].start()
    for s in range(sites):
        pltpu.make_async_copy(links_ref.at[0, s], raw.at[s], link_sem.at[s]).start()
    inputs[2].start()

    lane_site = lax.broadcasted_iota(jnp.int32, (1, width), 1) // rhs
    even = lane_site % 2 == 0

    def over_sites(x):
        shift = rhs
        while shift < width:
            x = x + pltpu.roll(x, shift, 1)
            shift *= 2
        return x

    row_site = lax.broadcasted_iota(jnp.int32, (sites * ks, width), 0) // ks
    diagonal = row_site == lax.broadcasted_iota(jnp.int32, (sites * ks, width), 1) // rhs

    def two_parts(a):
        hi = a.astype(BF16)
        return hi, (a - hi.astype(F32)).astype(BF16)


    def dot_parts(a, b):
        p = jnp.dot(a, b, preferred_element_type=F32)
        rows = a.shape[0] // 2
        return p[:rows, :width] + p[:rows, width:] + p[rows:, :width]

    def restrict():
        full = jnp.where(diagonal, dot_parts(prol_parts, weights[:comps]), 0.0)
        return functools.reduce(jnp.add, [full[s * ks : (s + 1) * ks] for s in range(sites)])

    def products(pairs, rows=1):
        packed = []
        for at in range(0, rows * sites, sites):
            row = jnp.zeros((1, width), F32)
            for i, (a, b) in enumerate(pairs[at : at + sites]):
                row = jnp.where(lane_site == i, over_sites(jnp.sum(a * b, axis=0, keepdims=True)), row)
            packed.append(row)
        return packed[0] if rows == 1 else jnp.concatenate(packed, axis=0)

    block = comps // sites

    def send_site(r, s, v):
        message = jnp.zeros((block, width), F32)
        for q in range(sites):
            moved = pltpu.roll(
                v[q * block : (q + 1) * block], lax.rem(q + sites - s, sites) * rhs, 1
            )
            message = jnp.where(lane_site == q, moved, message)
        outgoing[r, s] = message
        for side, to in ((0, left), (1, right)):
            pltpu.make_async_remote_copy(
                src_ref=outgoing.at[r, s],
                dst_ref=halo.at[r, side, s],
                send_sem=halo_send.at[r, side],
                recv_sem=halo_recv.at[r, side, s],
                device_id={"ta": to},
            ).start()

    def send_field(r, f):
        def one(s, carry):
            send_site(r, s, field[f])
            return carry

        lax.fori_loop(0, sites, one, 0)

    def near(k, src, dst):
        return [
            pltpu.make_async_remote_copy(
                src_ref=src,
                dst_ref=dst.at[side],
                send_sem=near_send.at[k, side],
                recv_sem=near_recv.at[k, side],
                device_id={"ta": to},
            )
            for side, to in ((0, left), (1, right))
        ]

    def exchange(k, value, staged, slots, send_sem, recv_sem):
        staged[k] = value
        slots[k, me] = value

        def one(d, carry):
            pltpu.make_async_remote_copy(
                src_ref=staged.at[k],
                dst_ref=slots.at[k, me],
                send_sem=send_sem.at[k],
                recv_sem=recv_sem.at[k],
                device_id={"ta": lax.rem(me + d, n)},
            ).start()
            return carry

        lax.fori_loop(1, n, one, 0)
        return pltpu.make_async_remote_copy(
            src_ref=slots.at[k, pl.ds(0, n - 1)],
            dst_ref=slots.at[k, pl.ds(0, n - 1)],
            send_sem=send_sem.at[k],
            recv_sem=recv_sem.at[k],
            device_id={"ta": right},
        )

    pending = []

    core, chips = lax.rem(me, 2), n // 2
    partner = me + 1 - 2 * core

    def gather_copy(k, blocks):
        return pltpu.make_async_remote_copy(
            src_ref=gather.at[k, core, blocks],
            dst_ref=gather.at[k, core, blocks],
            send_sem=gather_send.at[k],
            recv_sem=gather_recv.at[k],
            device_id={"ta": partner},
        )

    def share_copy(k):
        return pltpu.make_async_remote_copy(
            src_ref=gather.at[k, core],
            dst_ref=gather.at[k, core],
            send_sem=share_send.at[k],
            recv_sem=share_recv.at[k],
            device_id={"ta": partner},
        )

    def exchange_large(k, value):
        stage[k] = value
        gather[k, core, me // 2] = value

        def one(d, carry):
            pltpu.make_async_remote_copy(
                src_ref=stage.at[k],
                dst_ref=gather.at[k, core, me // 2],
                send_sem=gather_send.at[k],
                recv_sem=gather_recv.at[k],
                device_id={"ta": lax.rem(me + 2 * d, n)},
            ).start()
            return carry

        lax.fori_loop(1, chips, one, 0)

    def share_large(k):
        gather_copy(k, pl.ds(0, chips - 1)).wait_recv()
        share_copy(k).start()

    def exchange_small(k, value):
        c = exchange(k, value, small_stage, small, small_send, small_recv)
        pending.append(c)
        return c

    def load_weights(at, v):
        hi = v.astype(BF16)
        lo = (v - hi.astype(F32)).astype(BF16)
        weights[at * comps : (at + 1) * comps, :width] = hi
        weights[at * comps : (at + 1) * comps, width:] = lo

    def product(s, lo_k, hi_k):
        k = slice(lo_k * comps, hi_k * comps)
        p = jnp.dot(lcat[s, :comps, k], weights[k], preferred_element_type=F32)
        q = jnp.dot(lcat[s, comps:, k], weights[k, :width], preferred_element_type=F32)
        return p[:, :width] + p[:, width:] + q

    def load_inner(f):
        v = field[f]
        load_weights(0, v)
        load_weights(1, pltpu.roll(v, width // 2, 1))
        load_weights(2, jnp.where(even, pltpu.roll(v, width - rhs, 1), pltpu.roll(v, rhs, 1)))

    def inner():
        def site(s, carry):
            acc[...] = jnp.where(lane_site == s, product(s, 0, INNER_SUMS), acc[...])
            return carry

        lax.fori_loop(0, sites, site, 0, unroll=True)

    def outer(r, f, to, of_field, of_links, send=None):
        def site(s, carry):
            if r is not None:
                for side in range(2):
                    pltpu.make_async_remote_copy(
                        src_ref=outgoing.at[r, s],
                        dst_ref=halo.at[r, side, s],
                        send_sem=halo_send.at[r, side],
                        recv_sem=halo_recv.at[r, side, s],
                        device_id={"ta": left},
                    ).wait_recv()
                    m = halo[r, side, s]
                    load_weights(
                        INNER_SUMS + side,
                        jnp.concatenate(
                            [
                                pltpu.roll(m, lax.rem(s + sites - q, sites) * rhs, 1)
                                for q in range(sites)
                            ],
                            axis=0,
                        ),
                    )
            new = of_field * field[f] + of_links * (acc[...] + product(s, INNER_SUMS, len(LINK_SUMS)))
            field[to] = jnp.where(lane_site == s, new, field[to])
            if send is not None:
                send_site(send, s, new)
            return carry

        lax.fori_loop(0, sites, site, 0)

    def image_of(c):
        last = len(c) - 1
        inside = [(c[i] - c[i - 1]) / STEP for i in range(1, last + 1)]
        return [c[0] / STEP] + inside + [-c[last] / STEP]

    def factor_of(gram, c, d):
        gd = [
            functools.reduce(jnp.add, [gram(i, j) * d[j] for j in range(len(d))])
            for i in range(len(d))
        ]
        across = functools.reduce(jnp.add, [gd[i] * c[i] for i in range(len(c))])
        squared = functools.reduce(jnp.add, [gd[i] * d[i] for i in range(len(d))])
        return DAMPING * across / squared

    def advance(c, x, d, factor):
        x = [x[i] + factor * c[i] if i < len(c) else x[i] for i in range(SWEEPS)]
        return [c[i] - factor * d[i] if i < len(c) else -factor * d[i] for i in range(len(d))], x

    def sweeps(gram, count):
        c = [jnp.ones((1, width), F32)]
        x = [jnp.zeros((1, width), F32)] * SWEEPS
        for _ in range(count):
            d = image_of(c)
            c, x = advance(c, x, d, factor_of(gram, c, d))
        return c, x

    def combine(coefficients, fields):
        return functools.reduce(jnp.add, [a * field[f] for a, f in zip(coefficients, fields)])

    half = sites * ks
    inputs[0].wait()
    field[0] = source_in[0].reshape(width, comps).T
    pl.semaphore_wait(barrier, n - 1)
    send_field(0, 0)
    inputs[1].wait()
    prol_copies = near(0, prol_in.at[0], prol_halo)
    prol = prol_in[0].reshape(half, comps)
    prol_parts = jnp.concatenate(two_parts(prol), axis=0)

    def prepare(s, carry):
        pltpu.make_async_copy(links_ref.at[0, s], raw.at[s], link_sem.at[s]).wait()
        for at, members in enumerate(LINK_SUMS):
            total = functools.reduce(jnp.add, [raw[s, m] for m in members])
            hi = total.astype(BF16)
            lo = (total - hi.astype(F32)).astype(BF16)
            lcat[s, :comps, at * comps : (at + 1) * comps] = hi
            lcat[s, comps:, at * comps : (at + 1) * comps] = lo
        return carry

    lax.fori_loop(0, sites, prepare, 0)
    for k in range(SWEEPS + 1):
        load_inner(k)
        value = jnp.concatenate(
            [restrict(), products([(field[k], field[i]) for i in range(k + 1)])], axis=0
        )
        exchange_large(k, value)
        if k == SWEEPS:
            for copy in prol_copies:
                copy.start()
        inner()
        if k:
            share_large(k - 1)
        if k < SWEEPS:
            outer(k, k, k + 1, 1.0 - STEP, -STEP, k + 1 if k + 1 < SWEEPS else None)

    inputs[2].wait()
    inverse_parts = jnp.concatenate(two_parts(inverse_in[...]), axis=0)

    def total_of(slots, k, at, rows):
        return jnp.sum(slots.at[k][:, at : at + rows, :], axis=0)

    def unpack(total, i):
        row = total[i // sites : i // sites + 1]
        return over_sites(jnp.where(lane_site == i % sites, row, 0.0))

    def solve_coarse(coefficients):
        def spread(chip, carry):
            for half_chip in range(2):
                r = functools.reduce(
                    jnp.add,
                    [a * gather[k, half_chip, chip, :ks] for k, a in enumerate(coefficients)],
                )
                for s in range(sites):
                    hi, lo = two_parts(jnp.where(lane_site == s, r, 0.0))
                    row = ((2 * chip + half_chip) * sites + s) * ks
                    at = pl.ds(pl.multiple_of(row, ks), ks)
                    rall[at, :width] = hi
                    rall[at, width:] = lo
            return carry

        lax.fori_loop(0, chips, spread, 0)
        return over_sites(dot_parts(inverse_parts, rall[...]))

    def store_coarse(at, x):
        hi, lo = two_parts(x)
        xcat[at * half : (at + 1) * half, :width] = hi
        xcat[at * half : (at + 1) * half, width:] = lo

    grams = {}

    def gram(i, j):
        return grams[max(i, j), min(i, j)]

    def read_grams(k):
        share_copy(k).wait_recv()
        total = functools.reduce(jnp.add, [total_of(gather, (k, c), ks, 1) for c in range(2)])
        grams.update({(k, i): unpack(total, i) for i in range(k + 1)})

    for k in range(SWEEPS):
        read_grams(k)
    c, x = sweeps(gram, SWEEPS - 1)
    d = image_of(c)
    before = solve_coarse(c)
    xcat[3 * half :] = jnp.zeros((xcat.shape[0] - 3 * half, 2 * width), BF16)
    share_large(SWEEPS)
    read_grams(SWEEPS)
    factor = factor_of(gram, c, d)
    coarse = before - factor * solve_coarse(d)
    compact = functools.reduce(
        jnp.add,
        [jnp.where(lane_site == s, coarse[s * ks : (s + 1) * ks], 0.0) for s in range(sites)],
    )
    coarse_out[...] = compact
    coarse_copies = near(1, coarse_out, coarse_halo)
    for copy in coarse_copies:
        copy.start()
    c, x = advance(c, x, d, factor)
    store_coarse(0, coarse)
    send_field(SWEEPS, SWEEPS)
    for copy in prol_copies:
        copy.wait_recv()

    def columns_of(p):
        hi = p.astype(BF16).astype(F32)
        return jnp.concatenate([hi, p - hi], axis=0).T.astype(BF16)

    bases = [columns_of(p.reshape(half, comps)) for p in (prol, prol_halo[0], prol_halo[1])]
    vectors = jnp.concatenate([prol, prol], axis=0).T
    g_lane = lax.broadcasted_iota(jnp.int32, (1, 2 * half), 1)
    g_site, g_low = lax.rem(g_lane, half) // ks, g_lane < half

    def operate_on_bases(s, carry):
        def times(m, base):
            k = slice(m * comps, (m + 1) * comps)
            r = jnp.dot(lcat[s, :comps, k], base, preferred_element_type=F32)
            r = r + jnp.dot(lcat[s, comps:, k], base, preferred_element_type=F32)
            return r + pltpu.roll(r, half, 1)

        across = s + 1 - 2 * lax.rem(s, 2)
        own = jnp.where(g_site == s, vectors + times(0, bases[0]), 0.0)
        own = jnp.where(g_site == lax.rem(s + sites // 2, sites), times(1, bases[0]), own)
        own = jnp.where(g_site == across, times(2, bases[0]), own)
        ahead = jnp.where(g_site == s, times(3, bases[1]), 0.0)
        behind = jnp.where((g_site == s) & g_low, times(4, bases[2]), 0.0)
        for at, value in enumerate((jnp.where(g_low, own, ahead), behind)):
            hi, lo = two_parts(value)
            lanes = slice(at * 2 * half, (at + 1) * 2 * half)
            gcat[s, :comps, lanes] = hi
            gcat[s, comps:, lanes] = lo
        return carry

    lax.fori_loop(0, sites, operate_on_bases, 0)
    field[7] = combine(c, range(SWEEPS + 1))
    for side in range(2):
        coarse_copies[side].wait_recv()
        there = coarse_halo[side]
        store_coarse(
            1 + side,
            jnp.concatenate(
                [over_sites(jnp.where(lane_site == s, there, 0.0)) for s in range(sites)], axis=0
            ),
        )

    def operate_on_coarse(s, carry):
        p = jnp.dot(gcat[s, :comps], xcat[...], preferred_element_type=F32)
        q = jnp.dot(gcat[s, comps:], xcat[:, :width], preferred_element_type=F32)
        new = p[:, :width] + p[:, width:] + q
        field[6] = jnp.where(lane_site == s, new, field[6])
        send_site(4, s, new)
        return carry

    lax.fori_loop(0, sites, operate_on_coarse, 0)
    exchange_small(0, products([(field[6], field[7]), (field[6], field[6])], SMALL_ROWS))
    outer(SWEEPS, SWEEPS, SWEEPS + 1, 1.0 - STEP, -STEP)
    load_inner(6)
    inner()
    field[8] = combine(c, range(1, SWEEPS + 2))
    field[9] = combine(x, range(SWEEPS))
    field[5] = dot(prol.T, jnp.where(diagonal, coarse, 0.0))
    outer(4, 6, 14, 1.0 - STEP, -STEP)
    pending[-1].wait_recv()
    pair = total_of(small, 0, 0, SMALL_ROWS)
    g = unpack(pair, 0) / unpack(pair, 1)

    field[11] = field[8] - g * field[14]
    send_field(5, 11)
    field[10] = field[7] - g * field[6]
    field[9] = field[9] + g * field[5]
    load_inner(11)
    inner()
    outer(5, 11, 12, 1.0 - STEP, -STEP, 6)
    early = [(i, j) for i in range(3) for j in range(i + 1)]
    late = [(3, j) for j in range(4)]
    exchange_small(1, products([(field[10 + i], field[10 + j]) for i, j in early], SMALL_ROWS))
    load_inner(12)
    inner()
    outer(6, 12, 13, 1.0 - STEP, -STEP)
    exchange_small(2, products([(field[10 + i], field[10 + j]) for i, j in late], SMALL_ROWS))
    for r in range(halo.shape[0]):
        for side in range(2):
            pltpu.make_async_remote_copy(
                src_ref=outgoing.at[r],
                dst_ref=halo.at[r, side],
                send_sem=halo_send.at[r, side],
                recv_sem=halo_recv.at[r, side, 0],
                device_id={"ta": left},
            ).wait_send()
    for k in range(SWEEPS + 1):
        gather_copy(k, pl.ds(0, chips - 1)).wait_send()
        share_copy(k).wait_send()
    for copy in pending[:-1] + prol_copies + coarse_copies:
        copy.wait_send()
    pending[-2].wait_recv()
    total = total_of(small, 1, 0, SMALL_ROWS)
    grams = {pair: unpack(total, early.index(pair)) for pair in early}
    c, x = sweeps(gram, SWEEPS - 1)
    d = image_of(c)
    pending[-1].wait_recv()
    total = total_of(small, 2, 0, SMALL_ROWS)
    grams.update({pair: unpack(total, late.index(pair)) for pair in late})
    c, x = advance(c, x, d, factor_of(gram, c, d))
    residual_ref[...] = combine(c, range(10, 14))
    solution_ref[...] = field[9] + combine(x, range(10, 13))
    pending[-1].wait_send()


def turn(*refs):
    for column, row in zip(refs[:2], refs[2:]):
        row[0] = column[...].T.reshape(row.shape[1:])


def local(source, links, prolongator, coarse_inverse):
    n = lax.axis_size("ta")
    _, sites, rhs, comps = source.shape
    ks = prolongator.shape[2]
    width = sites * rhs
    sums = len(LINK_SUMS)
    vmem = pl.BlockSpec(memory_space=pltpu.VMEM)
    dma = pltpu.SemaphoreType.DMA
    columns = pl.pallas_call(
        functools.partial(kernel, n),
        out_shape=(jax.ShapeDtypeStruct((comps, width), F32),) * 2,
        in_specs=[pl.BlockSpec(memory_space=pl.ANY)] * 4,
        out_specs=(vmem, vmem),
        scratch_shapes=[
            pltpu.VMEM(source.shape, F32),
            pltpu.VMEM(prolongator.shape, F32),
            pltpu.VMEM(coarse_inverse.shape, F32),
            pltpu.VMEM(links.shape[1:], F32),
            pltpu.VMEM((sites, 2 * comps, sums * comps), BF16),
            pltpu.VMEM((sums * comps, 2 * width), BF16),
            pltpu.VMEM((15, comps, width), F32),
            pltpu.VMEM((7, sites, comps // sites, width), F32),
            pltpu.VMEM((7, 2, sites, comps // sites, width), F32),
            pltpu.VMEM((2, *prolongator.shape[1:]), F32),
            pltpu.VMEM((ks, width), F32),
            pltpu.VMEM((2, ks, width), F32),
            pltpu.VMEM((comps, width), F32),
            pltpu.VMEM((SWEEPS + 1, ks + 1, width), F32),
            pltpu.VMEM((SWEEPS + 1, 2, n // 2, ks + 1, width), F32),
            pltpu.VMEM((3, SMALL_ROWS, width), F32),
            pltpu.VMEM((3, n, SMALL_ROWS, width), F32),
            pltpu.VMEM((n * sites * ks, 2 * width), BF16),
            pltpu.VMEM((sites, 2 * comps, 4 * sites * ks), BF16),
            pltpu.VMEM((4 * sites * ks, 2 * width), BF16),
            dma((3,)),
            dma((sites,)),
            dma((7, 2)),
            dma((7, 2, sites)),
            dma((2, 2)),
            dma((2, 2)),
            dma((SWEEPS + 1,)),
            dma((SWEEPS + 1,)),
            dma((SWEEPS + 1,)),
            dma((SWEEPS + 1,)),
            dma((3,)),
            dma((3,)),
        ],
        compiler_params=pltpu.CompilerParams(
            collective_id=0, has_side_effects=True, vmem_limit_bytes=60 * 1024 * 1024
        ),
    )(source, links, prolongator, coarse_inverse)
    return pl.pallas_call(
        turn,
        out_shape=(jax.ShapeDtypeStruct(source.shape, F32),) * 2,
        in_specs=[vmem, vmem],
        out_specs=(vmem, vmem),
    )(*columns)


def solution(mesh):
    return jax.shard_map(
        local,
        mesh=mesh,
        in_specs=(
            P(("groups", "ta"), None, None, None),
            P("ta", None, None, None, None),
            P("ta", None, None, None),
            P("ta", None),
        ),
        out_specs=(P(("groups", "ta"), None, None, None), P(("groups", "ta"), None, None, None)),
        check_vma=False,
    )
```

```python
import functools

import jax
import jax.numpy as jnp
from jax import lax
from jax.experimental import pallas as pl
from jax.experimental.pallas import tpu as pltpu
from jax.sharding import PartitionSpec as P

LINK_SUMS = ((0, 3, 4), (5, 6), (7, 8), (1,), (2,))
INNER_SUMS = 3
DAMPING = 0.8
SWEEPS = 3
STEP = 0.8
F32 = jnp.float32
BF16 = jnp.bfloat16
SMALL_ROWS = 2


def dot(a, b):
    return jnp.dot(a, b, preferred_element_type=F32)


def dot_rows(a, b):
    return lax.dot_general(a, b, (((1,), (1,)), ((), ())), preferred_element_type=F32)


def two_parts(a):
    hi = a.astype(BF16)
    return hi, (a - hi.astype(F32)).astype(BF16)


def stacked_parts(a):
    return jnp.concatenate(two_parts(a), axis=0)


def fold(a):
    rows = a.shape[0] // 2
    return a[:rows] + a[rows:]


def kernel(
    n,
    source_ref,
    links_ref,
    prol_ref,
    inverse_ref,
    solution_ref,
    residual_ref,
    prol_in,
    inverse_in,
    raw,
    lcat,
    field,
    parts,
    acc,
    halo,
    prol_halo,
    prol_sites,
    images,
    coarse_out,
    coarse_halo,
    stage,
    gather,
    small_stage,
    small,
    rall,
    input_sem,
    link_sem,
    halo_send,
    halo_recv,
    near_send,
    near_recv,
    gather_send,
    gather_recv,
    share_send,
    share_recv,
    small_send,
    small_recv,
):
    me = lax.axis_index("ta")
    sites = links_ref.shape[1]
    width, comps = source_ref.shape
    rhs = width // sites
    half = prol_ref.shape[0]
    ks = half // sites
    sums = len(LINK_SUMS)
    right, left = lax.rem(me + 1, n), lax.rem(me + n - 1, n)

    barrier = pltpu.get_barrier_semaphore()

    def greet(d, carry):
        pl.semaphore_signal(barrier, inc=1, device_id={"ta": lax.rem(me + d, n)})
        return carry

    lax.fori_loop(1, n, greet, 0)
    inputs = [
        pltpu.make_async_copy(hbm, vmem, input_sem.at[i])
        for i, (hbm, vmem) in enumerate(
            ((source_ref, field.at[0]), (prol_ref, prol_in), (inverse_ref, inverse_in))
        )
    ]
    inputs[0].start()
    inputs[1].start()
    for s in range(sites):
        pltpu.make_async_copy(links_ref.at[0, s], raw.at[s], link_sem.at[s]).start()
    inputs[2].start()

    lane_site = lax.broadcasted_iota(jnp.int32, (1, width), 1) // rhs

    def over_sites(x):
        shift = rhs
        while shift < width:
            x = x + pltpu.roll(x, shift, 1)
            shift *= 2
        return x

    row_site = lax.broadcasted_iota(jnp.int32, (half, width), 0) // ks
    diagonal = row_site == lax.broadcasted_iota(jnp.int32, (half, width), 1) // rhs

    def rows_of(s, count=rhs):
        return pl.ds(pl.multiple_of(s * count, count), count)

    def dot_parts(a, b):
        p = dot(a, b)
        rows = a.shape[0] // 2
        return p[:rows, :width] + p[:rows, width:] + p[rows:, :width]

    def restrict():
        hi = jnp.concatenate([parts[s, :rhs] for s in range(sites)], axis=0)
        lo = jnp.concatenate([parts[s, rhs:] for s in range(sites)], axis=0)
        full = fold(dot_rows(prol_parts, hi)) + dot_rows(prol_parts[:half], lo)
        full = jnp.where(diagonal, full, 0.0)
        return functools.reduce(jnp.add, [full[s * ks : (s + 1) * ks] for s in range(sites)])

    def products(pairs, rows=1):
        packed = []
        for at in range(0, rows * sites, sites):
            sums_over = []
            for a, b in pairs[at : at + sites]:
                p = a * b
                p = functools.reduce(jnp.add, [p[s * rhs : (s + 1) * rhs] for s in range(sites)])
                sums_over.append(
                    functools.reduce(
                        jnp.add, [p[:, c : c + width] for c in range(0, comps, width)]
                    )
                )
            blank = [jnp.zeros((rhs, width), F32)] * (sites - len(sums_over))
            packed.append(
                jnp.sum(jnp.concatenate(sums_over + blank, axis=0).T, axis=0, keepdims=True)
            )
        return packed[0] if rows == 1 else jnp.concatenate(packed, axis=0)

    def columns(values):
        blank = [jnp.zeros((1, width), F32)] * (-len(values) % 8)
        turned = jnp.concatenate(list(values) + blank, axis=0).T
        return [turned[:, i : i + 1] for i in range(len(values))]

    def send_site(r, f, s):
        for side, to in ((0, left), (1, right)):
            pltpu.make_async_remote_copy(
                src_ref=field.at[f, rows_of(s)],
                dst_ref=halo.at[r, side, rows_of(s)],
                send_sem=halo_send.at[r, side],
                recv_sem=halo_recv.at[r, side, s],
                device_id={"ta": to},
            ).start()

    def send_field(r, f):
        for s in range(sites):
            send_site(r, f, s)

    def near(k, src, dst):
        return [
            pltpu.make_async_remote_copy(
                src_ref=src,
                dst_ref=dst.at[side],
                send_sem=near_send.at[k, side],
                recv_sem=near_recv.at[k, side],
                device_id={"ta": to},
            )
            for side, to in ((0, left), (1, right))
        ]

    pending = []

    core, chips = lax.rem(me, 2), n // 2
    partner = me + 1 - 2 * core

    def gather_copy(k, blocks):
        return pltpu.make_async_remote_copy(
            src_ref=gather.at[k, core, blocks],
            dst_ref=gather.at[k, core, blocks],
            send_sem=gather_send.at[k],
            recv_sem=gather_recv.at[k],
            device_id={"ta": partner},
        )

    def share_copy(k):
        return pltpu.make_async_remote_copy(
            src_ref=gather.at[k, core],
            dst_ref=gather.at[k, core],
            send_sem=share_send.at[k],
            recv_sem=share_recv.at[k],
            device_id={"ta": partner},
        )

    def exchange_large(k, value):
        stage[k] = value
        gather[k, core, me // 2] = value

        def one(d, carry):
            pltpu.make_async_remote_copy(
                src_ref=stage.at[k],
                dst_ref=gather.at[k, core, me // 2],
                send_sem=gather_send.at[k],
                recv_sem=gather_recv.at[k],
                device_id={"ta": lax.rem(me + 2 * d, n)},
            ).start()
            return carry

        lax.fori_loop(1, chips, one, 0)

    def share_large(k):
        gather_copy(k, pl.ds(0, chips - 1)).wait_recv()
        share_copy(k).start()

    def exchange_small(k, value):
        small_stage[k] = value
        small[k, me] = value

        def one(d, carry):
            pltpu.make_async_remote_copy(
                src_ref=small_stage.at[k],
                dst_ref=small.at[k, me],
                send_sem=small_send.at[k],
                recv_sem=small_recv.at[k],
                device_id={"ta": lax.rem(me + d, n)},
            ).start()
            return carry

        lax.fori_loop(1, n, one, 0)
        pending.append(
            pltpu.make_async_remote_copy(
                src_ref=small.at[k, pl.ds(0, n - 1)],
                dst_ref=small.at[k, pl.ds(0, n - 1)],
                send_sem=small_send.at[k],
                recv_sem=small_recv.at[k],
                device_id={"ta": right},
            )
        )

    def apply_links(s, vectors, first, last):
        k = slice(first * comps, last * comps)
        return fold(dot(vectors, lcat[s, 0, k]) + dot(vectors, lcat[s, 1, k]))

    def across(s):
        return (s + sites // 2) % sites, s ^ 1

    def load_inner(f):
        for s in range(sites):
            parts[s] = stacked_parts(field[f, s * rhs : (s + 1) * rhs])

    def inner():
        for s in range(sites):
            y, z = across(s)
            vectors = jnp.concatenate([parts[s], parts[y], parts[z]], axis=1)
            acc[s * rhs : (s + 1) * rhs] = apply_links(s, vectors, 0, INNER_SUMS)

    def outer(r, f, to, of_field, of_links, send=None, keep=False):
        def site(s, carry):
            for side in range(2):
                pltpu.make_async_remote_copy(
                    src_ref=field.at[0, rows_of(s)],
                    dst_ref=halo.at[r, side, rows_of(s)],
                    send_sem=halo_send.at[r, side],
                    recv_sem=halo_recv.at[r, side, s],
                    device_id={"ta": left},
                ).wait_recv()
            vectors = jnp.concatenate(
                [stacked_parts(halo[r, side, rows_of(s)]) for side in range(2)], axis=1
            )
            links = acc[rows_of(s)] + apply_links(s, vectors, INNER_SUMS, sums)
            new = of_field * field[f, rows_of(s)] + of_links * links
            field[to, rows_of(s)] = new
            if send is not None:
                send_site(send, to, s)
            if keep:
                parts[s] = stacked_parts(new)
            return carry

        lax.fori_loop(0, sites, site, 0)

    def image_of(c):
        last = len(c) - 1
        inside = [(c[i] - c[i - 1]) / STEP for i in range(1, last + 1)]
        return [c[0] / STEP] + inside + [-c[last] / STEP]

    def factor_of(gram, c, d):
        gd = [
            functools.reduce(jnp.add, [gram(i, j) * d[j] for j in range(len(d))])
            for i in range(len(d))
        ]
        across = functools.reduce(jnp.add, [gd[i] * c[i] for i in range(len(c))])
        squared = functools.reduce(jnp.add, [gd[i] * d[i] for i in range(len(d))])
        return DAMPING * across / squared

    def advance(c, x, d, factor):
        x = [x[i] + factor * c[i] if i < len(c) else x[i] for i in range(SWEEPS)]
        return [c[i] - factor * d[i] if i < len(c) else -factor * d[i] for i in range(len(d))], x

    def sweeps(gram, count):
        c = [jnp.ones((1, width), F32)]
        x = [jnp.zeros((1, width), F32)] * SWEEPS
        for _ in range(count):
            d = image_of(c)
            c, x = advance(c, x, d, factor_of(gram, c, d))
        return c, x

    def combine(coefficients, fields):
        return functools.reduce(jnp.add, [a * field[f] for a, f in zip(coefficients, fields)])

    images[...] = jnp.zeros(images.shape, BF16)
    inputs[0].wait()
    pl.semaphore_wait(barrier, n - 1)
    send_field(0, 0)
    load_inner(0)
    inputs[1].wait()
    prol_copies = near(0, prol_in, prol_halo)
    prol_parts = stacked_parts(prol_in[...])

    def prepare(s, carry):
        pltpu.make_async_copy(links_ref.at[0, s], raw.at[s], link_sem.at[s]).wait()
        for at, members in enumerate(LINK_SUMS):
            hi, lo = two_parts(functools.reduce(jnp.add, [raw[s, m] for m in members]).T)
            lcat[s, 0, at * comps : (at + 1) * comps] = hi
            lcat[s, 1, at * comps : (at + 1) * comps] = lo
        return carry

    lax.fori_loop(0, sites, prepare, 0)
    for k in range(SWEEPS + 1):
        value = jnp.concatenate(
            [restrict(), products([(field[k], field[i]) for i in range(k + 1)])], axis=0
        )
        exchange_large(k, value)
        if k == SWEEPS:
            for copy in prol_copies:
                copy.start()
        inner()
        if k:
            share_large(k - 1)
        if k < SWEEPS:
            outer(k, k, k + 1, 1.0 - STEP, -STEP, k + 1 if k + 1 < SWEEPS else None, True)

    inputs[2].wait()
    inverse_parts = stacked_parts(inverse_in[...])

    def total_of(slots, k, at, rows):
        return jnp.sum(slots.at[k][:, at : at + rows, :], axis=0)

    def unpack(total, i):
        row = total[i // sites : i // sites + 1]
        return over_sites(jnp.where(lane_site == i % sites, row, 0.0))

    def solve_coarse(coefficients):
        def spread(chip, carry):
            for half_chip in range(2):
                r = functools.reduce(
                    jnp.add,
                    [a * gather[k, half_chip, chip, :ks] for k, a in enumerate(coefficients)],
                )
                for s in range(sites):
                    hi, lo = two_parts(jnp.where(lane_site == s, r, 0.0))
                    row = ((2 * chip + half_chip) * sites + s) * ks
                    at = pl.ds(pl.multiple_of(row, ks), ks)
                    rall[at, :width] = hi
                    rall[at, width:] = lo
            return carry

        lax.fori_loop(0, chips, spread, 0)
        return over_sites(dot_parts(inverse_parts, rall[...]))

    grams = {}

    def gram(i, j):
        return grams[max(i, j), min(i, j)]

    def read_grams(k):
        share_copy(k).wait_recv()
        total = functools.reduce(jnp.add, [total_of(gather, (k, c), ks, 1) for c in range(2)])
        grams.update({(k, i): unpack(total, i) for i in range(k + 1)})

    for k in range(SWEEPS):
        read_grams(k)
    c, x = sweeps(gram, SWEEPS - 1)
    d = image_of(c)
    before = solve_coarse(c)
    share_large(SWEEPS)
    read_grams(SWEEPS)
    factor = factor_of(gram, c, d)
    coarse = before - factor * solve_coarse(d)
    coarse_out[...] = functools.reduce(
        jnp.add,
        [jnp.where(lane_site == s, coarse[s * ks : (s + 1) * ks], 0.0) for s in range(sites)],
    )
    coarse_copies = near(1, coarse_out, coarse_halo)
    for copy in coarse_copies:
        copy.start()
    send_field(SWEEPS, SWEEPS)
    c, x = advance(c, x, d, factor)
    turned = columns(c + x)
    c, x = turned[: len(c)], turned[len(c) :]
    field[7] = combine(c, range(SWEEPS + 1))

    for copy in prol_copies:
        copy.wait_recv()
    for at, block in enumerate((prol_in, prol_halo.at[0], prol_halo.at[1])):
        for s in range(sites):
            prol_sites[at, s] = stacked_parts(block[s * ks : (s + 1) * ks])
    for s in range(sites):
        y, z = across(s)
        terms = ((0, 0, s), (1, 0, y), (2, 0, z), (3, 1, s), (4, 2, s))
        for m, at, site in terms:
            value = apply_links(s, prol_sites[at, site], m, m + 1)
            if m == 0:
                value = value + prol_in[s * ks : (s + 1) * ks]
            row = at * half + site * ks
            images[s, 0, row : row + ks], images[s, 1, row : row + ks] = two_parts(value)

    there = [coarse]
    for side in range(2):
        coarse_copies[side].wait_recv()
        compact = coarse_halo[side]
        there += [over_sites(jnp.where(lane_site == s, compact, 0.0)) for s in range(sites)]
    there.append(jnp.zeros((images.shape[2] - 3 * half, width), F32))
    coarse_vectors = stacked_parts(jnp.concatenate(there, axis=0).T[:rhs])
    for s in range(sites):
        new = fold(dot(coarse_vectors, images[s, 0]) + dot(coarse_vectors, images[s, 1]))
        field[6, s * rhs : (s + 1) * rhs] = new
        send_site(4, 6, s)
        parts[s] = stacked_parts(new)
    exchange_small(0, products([(field[6], field[7]), (field[6], field[6])], SMALL_ROWS))
    outer(SWEEPS, SWEEPS, SWEEPS + 1, 1.0 - STEP, -STEP)
    inner()
    field[8] = combine(c, range(1, SWEEPS + 2))
    field[9] = combine(x, range(SWEEPS))
    spread_hi, spread_lo = two_parts(jnp.where(diagonal, coarse, 0.0).T)
    field[5] = (
        dot(spread_hi, prol_parts[:half])
        + dot(spread_lo, prol_parts[:half])
        + dot(spread_hi, prol_parts[half:])
    )
    outer(4, 6, 14, 1.0 - STEP, -STEP)
    pending[-1].wait_recv()
    pair = total_of(small, 0, 0, SMALL_ROWS)
    g = columns([unpack(pair, 0) / unpack(pair, 1)])[0]

    for s in range(sites):
        at = slice(s * rhs, (s + 1) * rhs)
        new = field[8, at] - g[at] * field[14, at]
        field[11, at] = new
        send_site(5, 11, s)
        parts[s] = stacked_parts(new)
    field[10] = field[7] - g * field[6]
    field[9] = field[9] + g * field[5]
    inner()
    outer(5, 11, 12, 1.0 - STEP, -STEP, 6, True)
    early = [(i, j) for i in range(3) for j in range(i + 1)]
    late = [(3, j) for j in range(4)]
    exchange_small(1, products([(field[10 + i], field[10 + j]) for i, j in early], SMALL_ROWS))
    inner()
    outer(6, 12, 13, 1.0 - STEP, -STEP)
    exchange_small(2, products([(field[10 + i], field[10 + j]) for i, j in late], SMALL_ROWS))
    for r in range(halo.shape[0]):
        for side in range(2):
            pltpu.make_async_remote_copy(
                src_ref=field.at[0],
                dst_ref=halo.at[r, side],
                send_sem=halo_send.at[r, side],
                recv_sem=halo_recv.at[r, side, 0],
                device_id={"ta": left},
            ).wait_send()
    for k in range(SWEEPS + 1):
        gather_copy(k, pl.ds(0, chips - 1)).wait_send()
        share_copy(k).wait_send()
    for copy in pending[:-1] + prol_copies + coarse_copies:
        copy.wait_send()
    pending[-2].wait_recv()
    total = total_of(small, 1, 0, SMALL_ROWS)
    grams = {pair: unpack(total, early.index(pair)) for pair in early}
    c, x = sweeps(gram, SWEEPS - 1)
    d = image_of(c)
    pending[-1].wait_recv()
    total = total_of(small, 2, 0, SMALL_ROWS)
    grams.update({pair: unpack(total, late.index(pair)) for pair in late})
    c, x = advance(c, x, d, factor_of(gram, c, d))
    turned = columns(c + x)
    residual_ref[...] = combine(turned[: len(c)], range(10, 14))
    solution_ref[...] = field[9] + combine(turned[len(c) :], range(10, 13))
    pending[-1].wait_send()


def hand_over(*refs):
    for got, out in zip(refs[:2], refs[2:]):
        out[...] = got[...]


def local(source, links, prolongator, coarse_inverse):
    n = lax.axis_size("ta")
    shape = source.shape
    _, sites, rhs, comps = shape
    ks = prolongator.shape[2]
    width, half = sites * rhs, sites * ks
    sums = len(LINK_SUMS)
    vmem = pl.BlockSpec(memory_space=pltpu.VMEM)
    dma = pltpu.SemaphoreType.DMA
    fields = (jax.ShapeDtypeStruct((width, comps), F32),) * 2
    results = pl.pallas_call(
        functools.partial(kernel, n),
        out_shape=fields,
        in_specs=[pl.BlockSpec(memory_space=pl.ANY)] * 4,
        out_specs=(vmem, vmem),
        scratch_shapes=[
            pltpu.VMEM((half, comps), F32),
            pltpu.VMEM(coarse_inverse.shape, F32),
            pltpu.VMEM(links.shape[1:], F32),
            pltpu.VMEM((sites, 2, sums * comps, comps), BF16),
            pltpu.VMEM((15, width, comps), F32),
            pltpu.VMEM((sites, 2 * rhs, comps), BF16),
            pltpu.VMEM((width, comps), F32),
            pltpu.VMEM((7, 2, width, comps), F32),
            pltpu.VMEM((2, half, comps), F32),
            pltpu.VMEM((3, sites, 2 * ks, comps), BF16),
            pltpu.VMEM((sites, 2, 4 * half, comps), BF16),
            pltpu.VMEM((ks, width), F32),
            pltpu.VMEM((2, ks, width), F32),
            pltpu.VMEM((SWEEPS + 1, ks + 1, width), F32),
            pltpu.VMEM((SWEEPS + 1, 2, n // 2, ks + 1, width), F32),
            pltpu.VMEM((3, SMALL_ROWS, width), F32),
            pltpu.VMEM((3, n, SMALL_ROWS, width), F32),
            pltpu.VMEM((n * half, 2 * width), BF16),
            dma((3,)),
            dma((sites,)),
            dma((7, 2)),
            dma((7, 2, sites)),
            dma((2, 2)),
            dma((2, 2)),
            dma((SWEEPS + 1,)),
            dma((SWEEPS + 1,)),
            dma((SWEEPS + 1,)),
            dma((SWEEPS + 1,)),
            dma((3,)),
            dma((3,)),
        ],
        compiler_params=pltpu.CompilerParams(
            collective_id=0, has_side_effects=True, vmem_limit_bytes=60 * 1024 * 1024
        ),
    )(
        source.reshape(width, comps),
        links,
        prolongator.reshape(half, comps),
        coarse_inverse,
    )
    results = pl.pallas_call(
        hand_over, out_shape=fields, in_specs=[vmem, vmem], out_specs=(vmem, vmem)
    )(*results)
    return tuple(r.reshape(shape) for r in results)


def solution(mesh):
    return jax.shard_map(
        local,
        mesh=mesh,
        in_specs=(
            P(("groups", "ta"), None, None, None),
            P("ta", None, None, None, None),
            P("ta", None, None, None),
            P("ta", None),
        ),
        out_specs=(P(("groups", "ta"), None, None, None), P(("groups", "ta"), None, None, None)),
        check_vma=False,
    )
```

```python
import functools

import jax
import jax.numpy as jnp
from jax import lax
from jax.experimental import pallas as pl
from jax.experimental.pallas import tpu as pltpu
from jax.sharding import PartitionSpec as P

LINK_SUMS = ((0, 3, 4), (5, 6), (7, 8), (1,), (2,))
INNER_SUMS = 3
DAMPING = 0.8
SWEEPS = 3
STEP = 0.8
F32 = jnp.float32
BF16 = jnp.bfloat16
SMALL_ROWS = 2


def dot(a, b):
    return jnp.dot(a, b, preferred_element_type=F32)


def dot_rows(a, b):
    return lax.dot_general(a, b, (((1,), (1,)), ((), ())), preferred_element_type=F32)


def two_parts(a):
    hi = a.astype(BF16)
    return hi, (a - hi.astype(F32)).astype(BF16)


def stacked_parts(a):
    return jnp.concatenate(two_parts(a), axis=0)


def fold(a):
    rows = a.shape[0] // 2
    return a[:rows] + a[rows:]


def kernel(
    n,
    source_ref,
    links_ref,
    prol_ref,
    inverse_ref,
    solution_ref,
    residual_ref,
    prol_in,
    inverse_in,
    raw,
    lcat,
    field,
    parts,
    acc,
    halo,
    prol_halo,
    prol_sites,
    images,
    coarse_out,
    coarse_halo,
    stage,
    gather,
    small_stage,
    small,
    rall,
    input_sem,
    link_sem,
    halo_send,
    halo_recv,
    near_send,
    near_recv,
    gather_send,
    gather_recv,
    share_send,
    share_recv,
    small_send,
    small_recv,
):
    me = lax.axis_index("ta")
    sites = links_ref.shape[1]
    width, comps = source_ref.shape
    rhs = width // sites
    half = prol_ref.shape[0]
    ks = half // sites
    sums = len(LINK_SUMS)
    right, left = lax.rem(me + 1, n), lax.rem(me + n - 1, n)

    barrier = pltpu.get_barrier_semaphore()

    def greet(d, carry):
        pl.semaphore_signal(barrier, inc=1, device_id={"ta": lax.rem(me + d, n)})
        return carry

    lax.fori_loop(1, n, greet, 0)
    inputs = [
        pltpu.make_async_copy(hbm, vmem, input_sem.at[i])
        for i, (hbm, vmem) in enumerate(
            ((source_ref, field.at[0]), (prol_ref, prol_in), (inverse_ref, inverse_in))
        )
    ]
    inputs[0].start()
    inputs[1].start()
    for s in range(sites):
        pltpu.make_async_copy(links_ref.at[0, s], raw.at[s], link_sem.at[s]).start()
    inputs[2].start()

    lane_site = lax.broadcasted_iota(jnp.int32, (1, width), 1) // rhs

    def over_sites(x):
        shift = rhs
        while shift < width:
            x = x + pltpu.roll(x, shift, 1)
            shift *= 2
        return x

    row_site = lax.broadcasted_iota(jnp.int32, (half, width), 0) // ks
    diagonal = row_site == lax.broadcasted_iota(jnp.int32, (half, width), 1) // rhs

    def rows_of(s, count=rhs):
        return pl.ds(pl.multiple_of(s * count, count), count)

    def dot_parts(a, b):
        p = dot(a, b)
        rows = a.shape[0] // 2
        return p[:rows, :width] + p[:rows, width:] + p[rows:, :width]

    def restrict():
        hi = jnp.concatenate([parts[s, :rhs] for s in range(sites)], axis=0)
        lo = jnp.concatenate([parts[s, rhs:] for s in range(sites)], axis=0)
        full = fold(dot_rows(prol_parts, hi)) + dot_rows(prol_parts[:half], lo)
        full = jnp.where(diagonal, full, 0.0)
        return functools.reduce(jnp.add, [full[s * ks : (s + 1) * ks] for s in range(sites)])

    def products(pairs, rows=1):
        packed = []
        for at in range(0, rows * sites, sites):
            sums_over = []
            for a, b in pairs[at : at + sites]:
                p = a * b
                p = functools.reduce(jnp.add, [p[s * rhs : (s + 1) * rhs] for s in range(sites)])
                sums_over.append(
                    functools.reduce(
                        jnp.add, [p[:, c : c + width] for c in range(0, comps, width)]
                    )
                )
            blank = [jnp.zeros((rhs, width), F32)] * (sites - len(sums_over))
            packed.append(
                jnp.sum(jnp.concatenate(sums_over + blank, axis=0).T, axis=0, keepdims=True)
            )
        return packed[0] if rows == 1 else jnp.concatenate(packed, axis=0)

    def columns(values):
        blank = [jnp.zeros((1, width), F32)] * (-len(values) % 8)
        turned = jnp.concatenate(list(values) + blank, axis=0).T
        return [turned[:, i : i + 1] for i in range(len(values))]

    def send_site(r, f, s):
        for side, to in ((0, left), (1, right)):
            pltpu.make_async_remote_copy(
                src_ref=field.at[f, rows_of(s)],
                dst_ref=halo.at[r, side, rows_of(s)],
                send_sem=halo_send.at[r, side],
                recv_sem=halo_recv.at[r, side, s],
                device_id={"ta": to},
            ).start()

    def send_field(r, f):
        for s in range(sites):
            send_site(r, f, s)

    def near(k, src, dst):
        return [
            pltpu.make_async_remote_copy(
                src_ref=src,
                dst_ref=dst.at[side],
                send_sem=near_send.at[k, side],
                recv_sem=near_recv.at[k, side],
                device_id={"ta": to},
            )
            for side, to in ((0, left), (1, right))
        ]

    pending = []

    core, chips = lax.rem(me, 2), n // 2
    partner = me + 1 - 2 * core

    def gather_copy(k, blocks):
        return pltpu.make_async_remote_copy(
            src_ref=gather.at[k, core, blocks],
            dst_ref=gather.at[k, core, blocks],
            send_sem=gather_send.at[k],
            recv_sem=gather_recv.at[k],
            device_id={"ta": partner},
        )

    def share_copy(k):
        return pltpu.make_async_remote_copy(
            src_ref=gather.at[k, core],
            dst_ref=gather.at[k, core],
            send_sem=share_send.at[k],
            recv_sem=share_recv.at[k],
            device_id={"ta": partner},
        )

    def exchange_large(k, value):
        stage[k] = value
        gather[k, core, me // 2] = value

        def one(d, carry):
            pltpu.make_async_remote_copy(
                src_ref=stage.at[k],
                dst_ref=gather.at[k, core, me // 2],
                send_sem=gather_send.at[k],
                recv_sem=gather_recv.at[k],
                device_id={"ta": lax.rem(me + 2 * d, n)},
            ).start()
            return carry

        lax.fori_loop(1, chips, one, 0)

    def share_large(k):
        gather_copy(k, pl.ds(0, chips - 1)).wait_recv()
        share_copy(k).start()

    def exchange_small(k, value):
        small_stage[k] = value
        small[k, me] = value

        def one(d, carry):
            pltpu.make_async_remote_copy(
                src_ref=small_stage.at[k],
                dst_ref=small.at[k, me],
                send_sem=small_send.at[k],
                recv_sem=small_recv.at[k],
                device_id={"ta": lax.rem(me + d, n)},
            ).start()
            return carry

        lax.fori_loop(1, n, one, 0)
        pending.append(
            pltpu.make_async_remote_copy(
                src_ref=small.at[k, pl.ds(0, n - 1)],
                dst_ref=small.at[k, pl.ds(0, n - 1)],
                send_sem=small_send.at[k],
                recv_sem=small_recv.at[k],
                device_id={"ta": right},
            )
        )

    def apply_links(s, vectors, first, last):
        k = slice(first * comps, last * comps)
        return fold(dot(vectors, lcat[s, 0, k]) + dot(vectors, lcat[s, 1, k]))

    def across(s):
        return (s + sites // 2) % sites, s ^ 1

    def load_inner(f):
        for s in range(sites):
            parts[s] = stacked_parts(field[f, s * rhs : (s + 1) * rhs])

    def inner():
        for s in range(sites):
            y, z = across(s)
            vectors = jnp.concatenate([parts[s], parts[y], parts[z]], axis=1)
            acc[s * rhs : (s + 1) * rhs] = apply_links(s, vectors, 0, INNER_SUMS)

    def outer(r, f, to, of_field, of_links, send=None, keep=False):
        def site(s, carry):
            for side in range(2):
                pltpu.make_async_remote_copy(
                    src_ref=field.at[0, rows_of(s)],
                    dst_ref=halo.at[r, side, rows_of(s)],
                    send_sem=halo_send.at[r, side],
                    recv_sem=halo_recv.at[r, side, s],
                    device_id={"ta": left},
                ).wait_recv()
            vectors = jnp.concatenate(
                [stacked_parts(halo[r, side, rows_of(s)]) for side in range(2)], axis=1
            )
            links = acc[rows_of(s)] + apply_links(s, vectors, INNER_SUMS, sums)
            new = of_field * field[f, rows_of(s)] + of_links * links
            field[to, rows_of(s)] = new
            if send is not None:
                send_site(send, to, s)
            if keep:
                parts[s] = stacked_parts(new)
            return carry

        lax.fori_loop(0, sites, site, 0)

    def image_of(c):
        last = len(c) - 1
        inside = [(c[i] - c[i - 1]) / STEP for i in range(1, last + 1)]
        return [c[0] / STEP] + inside + [-c[last] / STEP]

    def factor_of(gram, c, d):
        gd = [
            functools.reduce(jnp.add, [gram(i, j) * d[j] for j in range(len(d))])
            for i in range(len(d))
        ]
        across = functools.reduce(jnp.add, [gd[i] * c[i] for i in range(len(c))])
        squared = functools.reduce(jnp.add, [gd[i] * d[i] for i in range(len(d))])
        return DAMPING * across / squared

    def advance(c, x, d, factor):
        x = [x[i] + factor * c[i] if i < len(c) else x[i] for i in range(SWEEPS)]
        return [c[i] - factor * d[i] if i < len(c) else -factor * d[i] for i in range(len(d))], x

    def sweeps(gram, count):
        c = [jnp.ones((1, width), F32)]
        x = [jnp.zeros((1, width), F32)] * SWEEPS
        for _ in range(count):
            d = image_of(c)
            c, x = advance(c, x, d, factor_of(gram, c, d))
        return c, x

    def combine(coefficients, fields):
        return functools.reduce(jnp.add, [a * field[f] for a, f in zip(coefficients, fields)])

    images[...] = jnp.zeros(images.shape, BF16)
    inputs[0].wait()
    pl.semaphore_wait(barrier, n - 1)
    send_field(0, 0)
    load_inner(0)
    inputs[1].wait()
    prol_copies = near(0, prol_in, prol_halo)
    prol_parts = stacked_parts(prol_in[...])

    def prepare(s, carry):
        pltpu.make_async_copy(links_ref.at[0, s], raw.at[s], link_sem.at[s]).wait()
        for at, members in enumerate(LINK_SUMS):
            hi, lo = two_parts(functools.reduce(jnp.add, [raw[s, m] for m in members]).T)
            lcat[s, 0, at * comps : (at + 1) * comps] = hi
            lcat[s, 1, at * comps : (at + 1) * comps] = lo
        return carry

    lax.fori_loop(0, sites, prepare, 0)
    for k in range(SWEEPS + 1):
        value = jnp.concatenate(
            [restrict(), products([(field[k], field[i]) for i in range(k + 1)])], axis=0
        )
        exchange_large(k, value)
        if k == SWEEPS:
            for copy in prol_copies:
                copy.start()
        inner()
        if k:
            share_large(k - 1)
        if k < SWEEPS:
            outer(k, k, k + 1, 1.0 - STEP, -STEP, k + 1 if k + 1 < SWEEPS else None, True)

    inputs[2].wait()
    inverse_parts = stacked_parts(inverse_in[...])

    def total_of(slots, k, at, rows):
        return jnp.sum(slots.at[k][:, at : at + rows, :], axis=0)

    def unpack(total, i):
        row = total[i // sites : i // sites + 1]
        return over_sites(jnp.where(lane_site == i % sites, row, 0.0))

    def solve_coarse(coefficients):
        def spread(chip, carry):
            for half_chip in range(2):
                r = functools.reduce(
                    jnp.add,
                    [a * gather[k, half_chip, chip, :ks] for k, a in enumerate(coefficients)],
                )
                for s in range(sites):
                    hi, lo = two_parts(jnp.where(lane_site == s, r, 0.0))
                    row = ((2 * chip + half_chip) * sites + s) * ks
                    at = pl.ds(pl.multiple_of(row, ks), ks)
                    rall[at, :width] = hi
                    rall[at, width:] = lo
            return carry

        lax.fori_loop(0, chips, spread, 0)
        return over_sites(dot_parts(inverse_parts, rall[...]))

    grams = {}

    def gram(i, j):
        return grams[max(i, j), min(i, j)]

    def read_grams(k):
        share_copy(k).wait_recv()
        total = functools.reduce(jnp.add, [total_of(gather, (k, c), ks, 1) for c in range(2)])
        grams.update({(k, i): unpack(total, i) for i in range(k + 1)})

    for k in range(SWEEPS):
        read_grams(k)
    c, x = sweeps(gram, SWEEPS - 1)
    d = image_of(c)
    before = solve_coarse(c)
    share_large(SWEEPS)
    read_grams(SWEEPS)
    factor = factor_of(gram, c, d)
    coarse = before - factor * solve_coarse(d)
    coarse_out[...] = functools.reduce(
        jnp.add,
        [jnp.where(lane_site == s, coarse[s * ks : (s + 1) * ks], 0.0) for s in range(sites)],
    )
    coarse_copies = near(1, coarse_out, coarse_halo)
    for copy in coarse_copies:
        copy.start()
    send_field(SWEEPS, SWEEPS)
    c, x = advance(c, x, d, factor)
    turned = columns(c + x)
    c, x = turned[: len(c)], turned[len(c) :]
    field[7] = combine(c, range(SWEEPS + 1))

    for copy in prol_copies:
        copy.wait_recv()
    for at, block in enumerate((prol_in, prol_halo.at[0], prol_halo.at[1])):
        for s in range(sites):
            prol_sites[at, s] = stacked_parts(block[s * ks : (s + 1) * ks])
    for s in range(sites):
        y, z = across(s)
        terms = ((0, 0, s), (1, 0, y), (2, 0, z), (3, 1, s), (4, 2, s))
        for m, at, site in terms:
            value = apply_links(s, prol_sites[at, site], m, m + 1)
            if m == 0:
                value = value + prol_in[s * ks : (s + 1) * ks]
            row = at * half + site * ks
            images[s, 0, row : row + ks], images[s, 1, row : row + ks] = two_parts(value)

    there = [coarse]
    for side in range(2):
        coarse_copies[side].wait_recv()
        compact = coarse_halo[side]
        there += [over_sites(jnp.where(lane_site == s, compact, 0.0)) for s in range(sites)]
    there.append(jnp.zeros((images.shape[2] - 3 * half, width), F32))
    coarse_vectors = stacked_parts(jnp.concatenate(there, axis=0).T[:rhs])
    for s in range(sites):
        new = fold(dot(coarse_vectors, images[s, 0]) + dot(coarse_vectors, images[s, 1]))
        field[6, s * rhs : (s + 1) * rhs] = new
        send_site(4, 6, s)
        parts[s] = stacked_parts(new)
    exchange_small(0, products([(field[6], field[7]), (field[6], field[6])], SMALL_ROWS))
    outer(SWEEPS, SWEEPS, SWEEPS + 1, 1.0 - STEP, -STEP)
    inner()
    field[8] = combine(c, range(1, SWEEPS + 2))
    field[9] = combine(x, range(SWEEPS))
    spread_hi, spread_lo = two_parts(jnp.where(diagonal, coarse, 0.0).T)
    field[5] = (
        dot(spread_hi, prol_parts[:half])
        + dot(spread_lo, prol_parts[:half])
        + dot(spread_hi, prol_parts[half:])
    )
    outer(4, 6, 14, 1.0 - STEP, -STEP)
    pending[-1].wait_recv()
    pair = total_of(small, 0, 0, SMALL_ROWS)
    g = columns([unpack(pair, 0) / unpack(pair, 1)])[0]

    for s in range(sites):
        at = slice(s * rhs, (s + 1) * rhs)
        new = field[8, at] - g[at] * field[14, at]
        field[11, at] = new
        send_site(5, 11, s)
        parts[s] = stacked_parts(new)
    field[10] = field[7] - g * field[6]
    field[9] = field[9] + g * field[5]
    inner()
    outer(5, 11, 12, 1.0 - STEP, -STEP, 6, True)
    early = [(i, j) for i in range(3) for j in range(i + 1)]
    late = [(3, j) for j in range(4)]
    exchange_small(1, products([(field[10 + i], field[10 + j]) for i, j in early], SMALL_ROWS))
    inner()
    outer(6, 12, 13, 1.0 - STEP, -STEP)
    exchange_small(2, products([(field[10 + i], field[10 + j]) for i, j in late], SMALL_ROWS))
    for r in range(halo.shape[0]):
        for side in range(2):
            pltpu.make_async_remote_copy(
                src_ref=field.at[0],
                dst_ref=halo.at[r, side],
                send_sem=halo_send.at[r, side],
                recv_sem=halo_recv.at[r, side, 0],
                device_id={"ta": left},
            ).wait_send()
    for k in range(SWEEPS + 1):
        gather_copy(k, pl.ds(0, chips - 1)).wait_send()
        share_copy(k).wait_send()
    for copy in pending[:-1] + prol_copies + coarse_copies:
        copy.wait_send()
    pending[-2].wait_recv()
    total = total_of(small, 1, 0, SMALL_ROWS)
    grams = {pair: unpack(total, early.index(pair)) for pair in early}
    c, x = sweeps(gram, SWEEPS - 1)
    d = image_of(c)
    pending[-1].wait_recv()
    total = total_of(small, 2, 0, SMALL_ROWS)
    grams.update({pair: unpack(total, late.index(pair)) for pair in late})
    c, x = advance(c, x, d, factor_of(gram, c, d))
    turned = columns(c + x)
    residual_ref[...] = combine(turned[: len(c)], range(10, 14))
    solution_ref[...] = field[9] + combine(turned[len(c) :], range(10, 13))
    pending[-1].wait_send()


def hand_over(*refs):
    copies = [pltpu.make_async_copy(refs[i], refs[2 + i], refs[4].at[i]) for i in range(2)]
    for copy in copies:
        copy.start()
    for copy in copies:
        copy.wait()


def local(source, links, prolongator, coarse_inverse):
    n = lax.axis_size("ta")
    shape = source.shape
    _, sites, rhs, comps = shape
    ks = prolongator.shape[2]
    width, half = sites * rhs, sites * ks
    sums = len(LINK_SUMS)
    vmem = pl.BlockSpec(memory_space=pltpu.VMEM)
    dma = pltpu.SemaphoreType.DMA
    fields = (jax.ShapeDtypeStruct((width, comps), F32),) * 2
    results = pl.pallas_call(
        functools.partial(kernel, n),
        out_shape=(pltpu.VMEM((width, comps), F32),) * 2,
        in_specs=[pl.BlockSpec(memory_space=pl.ANY)] * 4,
        out_specs=(vmem, vmem),
        scratch_shapes=[
            pltpu.VMEM((half, comps), F32),
            pltpu.VMEM(coarse_inverse.shape, F32),
            pltpu.VMEM(links.shape[1:], F32),
            pltpu.VMEM((sites, 2, sums * comps, comps), BF16),
            pltpu.VMEM((15, width, comps), F32),
            pltpu.VMEM((sites, 2 * rhs, comps), BF16),
            pltpu.VMEM((width, comps), F32),
            pltpu.VMEM((7, 2, width, comps), F32),
            pltpu.VMEM((2, half, comps), F32),
            pltpu.VMEM((3, sites, 2 * ks, comps), BF16),
            pltpu.VMEM((sites, 2, 4 * half, comps), BF16),
            pltpu.VMEM((ks, width), F32),
            pltpu.VMEM((2, ks, width), F32),
            pltpu.VMEM((SWEEPS + 1, ks + 1, width), F32),
            pltpu.VMEM((SWEEPS + 1, 2, n // 2, ks + 1, width), F32),
            pltpu.VMEM((3, SMALL_ROWS, width), F32),
            pltpu.VMEM((3, n, SMALL_ROWS, width), F32),
            pltpu.VMEM((n * half, 2 * width), BF16),
            dma((3,)),
            dma((sites,)),
            dma((7, 2)),
            dma((7, 2, sites)),
            dma((2, 2)),
            dma((2, 2)),
            dma((SWEEPS + 1,)),
            dma((SWEEPS + 1,)),
            dma((SWEEPS + 1,)),
            dma((SWEEPS + 1,)),
            dma((3,)),
            dma((3,)),
        ],
        compiler_params=pltpu.CompilerParams(
            collective_id=0, has_side_effects=True, vmem_limit_bytes=60 * 1024 * 1024
        ),
    )(
        source.reshape(width, comps),
        links,
        prolongator.reshape(half, comps),
        coarse_inverse,
    )
    results = pl.pallas_call(
        hand_over, out_shape=fields, in_specs=[vmem] * 2,
        out_specs=(pl.BlockSpec(memory_space=pl.ANY),) * 2, scratch_shapes=[dma((2,))],
        compiler_params=pltpu.CompilerParams(vmem_limit_bytes=1024 * 1024),
    )(*[pltpu.with_memory_space_constraint(r, pltpu.VMEM) for r in results])
    return tuple(r.reshape(shape) for r in results)


def solution(mesh):
    return jax.shard_map(
        local,
        mesh=mesh,
        in_specs=(
            P(("groups", "ta"), None, None, None),
            P("ta", None, None, None, None),
            P("ta", None, None, None),
            P("ta", None),
        ),
        out_specs=(P(("groups", "ta"), None, None, None), P(("groups", "ta"), None, None, None)),
        check_vma=False,
    )
```

```python
import functools

import jax
import jax.numpy as jnp
from jax import lax
from jax.experimental import pallas as pl
from jax.experimental.pallas import tpu as pltpu
from jax.sharding import PartitionSpec as P

LINK_SUMS = ((0, 3, 4), (5, 6), (7, 8), (1,), (2,))
INNER_SUMS = 3
DAMPING = 0.8
SWEEPS = 3
STEP = 0.8
F32 = jnp.float32
BF16 = jnp.bfloat16
SMALL_ROWS = 2


def dot(a, b):
    return jnp.dot(a, b, preferred_element_type=F32)


def dot_rows(a, b):
    return lax.dot_general(a, b, (((1,), (1,)), ((), ())), preferred_element_type=F32)


def two_parts(a):
    hi = a.astype(BF16)
    return hi, (a - hi.astype(F32)).astype(BF16)


def stacked_parts(a):
    return jnp.concatenate(two_parts(a), axis=0)


def fold(a):
    rows = a.shape[0] // 2
    return a[:rows] + a[rows:]


def kernel(
    n,
    source_ref,
    links_ref,
    prol_ref,
    inverse_ref,
    solution_ref,
    residual_ref,
    prol_in,
    inverse_in,
    raw,
    lcat,
    field,
    parts,
    acc,
    halo,
    prol_halo,
    prol_sites,
    images,
    coarse_out,
    coarse_halo,
    acc_coarse,
    stage,
    gather,
    small_stage,
    small,
    rall,
    input_sem,
    link_sem,
    halo_send,
    halo_recv,
    near_send,
    near_recv,
    gather_send,
    gather_recv,
    share_send,
    share_recv,
    small_send,
    small_recv,
):
    me = lax.axis_index("ta")
    sites = links_ref.shape[1]
    width, comps = source_ref.shape
    rhs = width // sites
    half = prol_ref.shape[0]
    ks = half // sites
    sums = len(LINK_SUMS)
    right, left = lax.rem(me + 1, n), lax.rem(me + n - 1, n)
    upper = me >= n // 2

    def far_first(start, d):
        return lax.rem(start + jnp.where(upper, d, n - d), n)

    barrier = pltpu.get_barrier_semaphore()

    def greet(d, carry):
        pl.semaphore_signal(barrier, inc=1, device_id={"ta": lax.rem(me + d, n)})
        return carry

    lax.fori_loop(1, n, greet, 0)
    inputs = [
        pltpu.make_async_copy(hbm, vmem, input_sem.at[i])
        for i, (hbm, vmem) in enumerate(
            ((source_ref, field.at[0]), (prol_ref, prol_in), (inverse_ref, inverse_in))
        )
    ]
    inputs[0].start()
    inputs[1].start()
    for s in range(sites):
        pltpu.make_async_copy(links_ref.at[0, s], raw.at[s], link_sem.at[s]).start()
    inputs[2].start()

    lane_site = lax.broadcasted_iota(jnp.int32, (1, width), 1) // rhs

    def over_sites(x):
        shift = rhs
        while shift < width:
            x = x + pltpu.roll(x, shift, 1)
            shift *= 2
        return x

    row_site = lax.broadcasted_iota(jnp.int32, (half, width), 0) // ks
    diagonal = row_site == lax.broadcasted_iota(jnp.int32, (half, width), 1) // rhs

    def rows_of(s, count=rhs):
        return pl.ds(pl.multiple_of(s * count, count), count)

    def dot_parts(a, b):
        p = dot(a, b)
        rows = a.shape[0] // 2
        return p[:rows, :width] + p[:rows, width:] + p[rows:, :width]

    def restrict():
        hi = jnp.concatenate([parts[s, :rhs] for s in range(sites)], axis=0)
        lo = jnp.concatenate([parts[s, rhs:] for s in range(sites)], axis=0)
        full = fold(dot_rows(prol_parts, hi)) + dot_rows(prol_parts[:half], lo)
        full = jnp.where(diagonal, full, 0.0)
        return functools.reduce(jnp.add, [full[s * ks : (s + 1) * ks] for s in range(sites)])

    def products(pairs, rows=1):
        packed = []
        for at in range(0, rows * sites, sites):
            sums_over = []
            for a, b in pairs[at : at + sites]:
                p = a * b
                p = functools.reduce(jnp.add, [p[s * rhs : (s + 1) * rhs] for s in range(sites)])
                sums_over.append(
                    functools.reduce(
                        jnp.add, [p[:, c : c + width] for c in range(0, comps, width)]
                    )
                )
            blank = [jnp.zeros((rhs, width), F32)] * (sites - len(sums_over))
            packed.append(
                jnp.sum(jnp.concatenate(sums_over + blank, axis=0).T, axis=0, keepdims=True)
            )
        return packed[0] if rows == 1 else jnp.concatenate(packed, axis=0)

    def columns(values):
        blank = [jnp.zeros((1, width), F32)] * (-len(values) % 8)
        turned = jnp.concatenate(list(values) + blank, axis=0).T
        return [turned[:, i : i + 1] for i in range(len(values))]

    def send_site(r, f, s):
        for side, to in ((0, left), (1, right)):
            pltpu.make_async_remote_copy(
                src_ref=field.at[f, rows_of(s)],
                dst_ref=halo.at[r, side, rows_of(s)],
                send_sem=halo_send.at[r, side],
                recv_sem=halo_recv.at[r, side, s],
                device_id={"ta": to},
            ).start()

    def send_field(r, f):
        for s in range(sites):
            send_site(r, f, s)

    def near(k, src, dst):
        return [
            pltpu.make_async_remote_copy(
                src_ref=src,
                dst_ref=dst.at[side],
                send_sem=near_send.at[k, side],
                recv_sem=near_recv.at[k, side],
                device_id={"ta": to},
            )
            for side, to in ((0, left), (1, right))
        ]

    pending = []

    core, chips = lax.rem(me, 2), n // 2
    partner = me + 1 - 2 * core

    def gather_copy(k, blocks):
        return pltpu.make_async_remote_copy(
            src_ref=gather.at[k, core, blocks],
            dst_ref=gather.at[k, core, blocks],
            send_sem=gather_send.at[k],
            recv_sem=gather_recv.at[k],
            device_id={"ta": partner},
        )

    def share_copy(k):
        return pltpu.make_async_remote_copy(
            src_ref=gather.at[k, core],
            dst_ref=gather.at[k, core],
            send_sem=share_send.at[k],
            recv_sem=share_recv.at[k],
            device_id={"ta": partner},
        )

    def exchange_large(k, value):
        stage[k] = value
        gather[k, core, me // 2] = value

        def send(to, send_sem, recv_sem):
            pltpu.make_async_remote_copy(
                src_ref=stage.at[k],
                dst_ref=gather.at[k, core, me // 2],
                send_sem=send_sem.at[k],
                recv_sem=recv_sem.at[k],
                device_id={"ta": to},
            ).start()

        def one(d, carry):
            send(far_first(me, 2 * d), gather_send, gather_recv)
            if k == SWEEPS:
                send(far_first(partner, 2 * d), share_send, share_recv)
            return carry

        lax.fori_loop(1, chips, one, 0)
        if k == SWEEPS:
            send(partner, share_send, share_recv)

    def share_large(k):
        gather_copy(k, pl.ds(0, chips - 1)).wait_recv()
        if k < SWEEPS:
            share_copy(k).start()

    def exchange_small(k, value):
        small_stage[k] = value
        small[k, me] = value

        def one(d, carry):
            pltpu.make_async_remote_copy(
                src_ref=small_stage.at[k],
                dst_ref=small.at[k, me],
                send_sem=small_send.at[k],
                recv_sem=small_recv.at[k],
                device_id={"ta": far_first(me, d)},
            ).start()
            return carry

        lax.fori_loop(1, n, one, 0)
        pending.append(
            pltpu.make_async_remote_copy(
                src_ref=small.at[k, pl.ds(0, n - 1)],
                dst_ref=small.at[k, pl.ds(0, n - 1)],
                send_sem=small_send.at[k],
                recv_sem=small_recv.at[k],
                device_id={"ta": right},
            )
        )

    def apply_links(s, vectors, first, last):
        k = slice(first * comps, last * comps)
        return fold(dot(vectors, lcat[s, 0, k]) + dot(vectors, lcat[s, 1, k]))

    def across(s):
        return (s + sites // 2) % sites, s ^ 1

    def load_inner(f):
        for s in range(sites):
            parts[s] = stacked_parts(field[f, s * rhs : (s + 1) * rhs])

    def inner(send=None):
        for s in range(sites):
            if send is not None:
                send_site(*send, s)
            y, z = across(s)
            vectors = jnp.concatenate([parts[s], parts[y], parts[z]], axis=1)
            acc[s * rhs : (s + 1) * rhs] = apply_links(s, vectors, 0, INNER_SUMS)

    def outer(r, f, to, of_field, of_links, send=None, keep=False):
        def site(s, carry):
            for side in range(2):
                pltpu.make_async_remote_copy(
                    src_ref=field.at[0, rows_of(s)],
                    dst_ref=halo.at[r, side, rows_of(s)],
                    send_sem=halo_send.at[r, side],
                    recv_sem=halo_recv.at[r, side, s],
                    device_id={"ta": left},
                ).wait_recv()
            vectors = jnp.concatenate(
                [stacked_parts(halo[r, side, rows_of(s)]) for side in range(2)], axis=1
            )
            links = acc[rows_of(s)] + apply_links(s, vectors, INNER_SUMS, sums)
            new = of_field * field[f, rows_of(s)] + of_links * links
            field[to, rows_of(s)] = new
            if send is not None:
                send_site(send, to, s)
            if keep:
                parts[s] = stacked_parts(new)
            return carry

        lax.fori_loop(0, sites, site, 0)

    def image_of(c):
        last = len(c) - 1
        inside = [(c[i] - c[i - 1]) / STEP for i in range(1, last + 1)]
        return [c[0] / STEP] + inside + [-c[last] / STEP]

    def factor_of(gram, c, d):
        gd = [
            functools.reduce(jnp.add, [gram(i, j) * d[j] for j in range(len(d))])
            for i in range(len(d))
        ]
        across = functools.reduce(jnp.add, [gd[i] * c[i] for i in range(len(c))])
        squared = functools.reduce(jnp.add, [gd[i] * d[i] for i in range(len(d))])
        return DAMPING * across / squared

    def advance(c, x, d, factor):
        x = [x[i] + factor * c[i] if i < len(c) else x[i] for i in range(SWEEPS)]
        return [c[i] - factor * d[i] if i < len(c) else -factor * d[i] for i in range(len(d))], x

    def sweeps(gram, count):
        c = [jnp.ones((1, width), F32)]
        x = [jnp.zeros((1, width), F32)] * SWEEPS
        for _ in range(count):
            d = image_of(c)
            c, x = advance(c, x, d, factor_of(gram, c, d))
        return c, x

    def combine(coefficients, fields):
        return functools.reduce(jnp.add, [a * field[f] for a, f in zip(coefficients, fields)])

    images[...] = jnp.zeros(images.shape, BF16)
    inputs[0].wait()
    pl.semaphore_wait(barrier, n - 1)
    send_field(0, 0)
    load_inner(0)
    inputs[1].wait()
    prol_copies = near(0, prol_in, prol_halo)
    prol_parts = stacked_parts(prol_in[...])

    def prepare(s, carry):
        pltpu.make_async_copy(links_ref.at[0, s], raw.at[s], link_sem.at[s]).wait()
        for at, members in enumerate(LINK_SUMS):
            hi, lo = two_parts(functools.reduce(jnp.add, [raw[s, m] for m in members]).T)
            lcat[s, 0, at * comps : (at + 1) * comps] = hi
            lcat[s, 1, at * comps : (at + 1) * comps] = lo
        return carry

    lax.fori_loop(0, sites, prepare, 0)
    for k in range(SWEEPS + 1):
        value = jnp.concatenate(
            [restrict(), products([(field[k], field[i]) for i in range(k + 1)])], axis=0
        )
        exchange_large(k, value)
        if k == SWEEPS:
            send_field(k, k)
            for copy in prol_copies:
                copy.start()
        inner()
        if k:
            share_large(k - 1)
        if k < SWEEPS:
            outer(k, k, k + 1, 1.0 - STEP, -STEP, k + 1 if k + 1 < SWEEPS else None, True)

    inputs[2].wait()
    inverse_parts = stacked_parts(inverse_in[...])

    def total_of(slots, k, at, rows):
        return jnp.sum(slots.at[k][:, at : at + rows, :], axis=0)

    def unpack(total, i):
        row = total[i // sites : i // sites + 1]
        return over_sites(jnp.where(lane_site == i % sites, row, 0.0))

    def solve_coarse(coefficients):
        def spread(chip, carry):
            for half_chip in range(2):
                r = functools.reduce(
                    jnp.add,
                    [a * gather[k, half_chip, chip, :ks] for k, a in enumerate(coefficients)],
                )
                for s in range(sites):
                    hi, lo = two_parts(jnp.where(lane_site == s, r, 0.0))
                    row = ((2 * chip + half_chip) * sites + s) * ks
                    at = pl.ds(pl.multiple_of(row, ks), ks)
                    rall[at, :width] = hi
                    rall[at, width:] = lo
            return carry

        lax.fori_loop(0, chips, spread, 0, unroll=4)
        return over_sites(dot_parts(inverse_parts, rall[...]))

    grams = {}

    def gram(i, j):
        return grams[max(i, j), min(i, j)]

    def read_grams(k):
        share_copy(k).wait_recv()
        total = functools.reduce(jnp.add, [total_of(gather, (k, c), ks, 1) for c in range(2)])
        grams.update({(k, i): unpack(total, i) for i in range(k + 1)})

    for k in range(SWEEPS):
        read_grams(k)
    c, x = sweeps(gram, SWEEPS - 1)
    d = image_of(c)
    before = solve_coarse(c)
    share_large(SWEEPS)
    read_grams(SWEEPS)
    factor = factor_of(gram, c, d)
    coarse = before - factor * solve_coarse(d)
    coarse_out[...] = jnp.concatenate([coarse, jnp.zeros((width - half, width), F32)], axis=0).T[:rhs]
    coarse_copies = near(1, coarse_out, coarse_halo)
    for copy in coarse_copies:
        copy.start()
    c, x = advance(c, x, d, factor)
    turned = columns(c + x)
    c, x = turned[: len(c)], turned[len(c) :]
    field[7] = combine(c, range(SWEEPS + 1))

    for copy in prol_copies:
        copy.wait_recv()
    for at, block in enumerate((prol_in, prol_halo.at[0], prol_halo.at[1])):
        for s in range(sites):
            prol_sites[at, s] = stacked_parts(block[s * ks : (s + 1) * ks])
    for s in range(sites):
        y, z = across(s)
        terms = ((0, 0, s), (1, 0, y), (2, 0, z), (3, 1, s), (4, 2, s))
        for m, at, site in terms:
            value = apply_links(s, prol_sites[at, site], m, m + 1)
            if m == 0:
                value = value + prol_in[s * ks : (s + 1) * ks]
            row = at * half + site * ks
            images[s, 0, row : row + ks], images[s, 1, row : row + ks] = two_parts(value)

    def vectors_of(block):
        return stacked_parts(block[:, :half])

    def part_of(s, vectors, at):
        k = slice(at * half, (at + 1) * half)
        return fold(dot(vectors, images[s, 0, k]) + dot(vectors, images[s, 1, k]))

    own = vectors_of(coarse_out[...])
    for s in range(sites):
        acc_coarse[s * rhs : (s + 1) * rhs] = part_of(s, own, 0)
    for copy in coarse_copies:
        copy.wait_recv()
    around = jnp.concatenate([vectors_of(coarse_halo[side]) for side in range(2)], axis=1)
    for s in range(sites):
        k = slice(half, 3 * half)
        links = fold(dot(around, images[s, 0, k]) + dot(around, images[s, 1, k]))
        new = acc_coarse[s * rhs : (s + 1) * rhs] + links
        field[6, s * rhs : (s + 1) * rhs] = new
        send_site(4, 6, s)
        parts[s] = stacked_parts(new)
    exchange_small(0, products([(field[6], field[7]), (field[6], field[6])], SMALL_ROWS))
    outer(SWEEPS, SWEEPS, SWEEPS + 1, 1.0 - STEP, -STEP)
    inner()
    field[8] = combine(c, range(1, SWEEPS + 2))
    field[9] = combine(x, range(SWEEPS))
    spread_hi, spread_lo = two_parts(jnp.where(diagonal, coarse, 0.0).T)
    field[5] = (
        dot(spread_hi, prol_parts[:half])
        + dot(spread_lo, prol_parts[:half])
        + dot(spread_hi, prol_parts[half:])
    )
    outer(4, 6, 14, 1.0 - STEP, -STEP)
    pending[-1].wait_recv()
    pair = total_of(small, 0, 0, SMALL_ROWS)
    g = columns([unpack(pair, 0) / unpack(pair, 1)])[0]

    for s in range(sites):
        at = slice(s * rhs, (s + 1) * rhs)
        new = field[8, at] - g[at] * field[14, at]
        field[11, at] = new
        parts[s] = stacked_parts(new)
    inner((5, 11))
    field[10] = field[7] - g * field[6]
    field[9] = field[9] + g * field[5]
    outer(5, 11, 12, 1.0 - STEP, -STEP, 6, True)
    early = [(i, j) for i in range(3) for j in range(i + 1)]
    late = [(3, j) for j in range(4)]
    exchange_small(1, products([(field[10 + i], field[10 + j]) for i, j in early], SMALL_ROWS))
    inner()
    outer(6, 12, 13, 1.0 - STEP, -STEP)
    exchange_small(2, products([(field[10 + i], field[10 + j]) for i, j in late], SMALL_ROWS))
    for r in range(halo.shape[0]):
        for side in range(2):
            pltpu.make_async_remote_copy(
                src_ref=field.at[0],
                dst_ref=halo.at[r, side],
                send_sem=halo_send.at[r, side],
                recv_sem=halo_recv.at[r, side, 0],
                device_id={"ta": left},
            ).wait_send()
    for k in range(SWEEPS + 1):
        gather_copy(k, pl.ds(0, chips - 1)).wait_send()
        share_copy(k).wait_send()
    for copy in pending[:-1] + prol_copies + coarse_copies:
        copy.wait_send()
    pending[-2].wait_recv()
    total = total_of(small, 1, 0, SMALL_ROWS)
    grams = {pair: unpack(total, early.index(pair)) for pair in early}
    c, x = sweeps(gram, SWEEPS - 1)
    d = image_of(c)
    pending[-1].wait_recv()
    total = total_of(small, 2, 0, SMALL_ROWS)
    grams.update({pair: unpack(total, late.index(pair)) for pair in late})
    c, x = advance(c, x, d, factor_of(gram, c, d))
    turned = columns(c + x)
    residual_ref[...] = combine(turned[: len(c)], range(10, 14))
    solution_ref[...] = field[9] + combine(turned[len(c) :], range(10, 13))
    pending[-1].wait_send()


def hand_over(*refs):
    copies = [pltpu.make_async_copy(refs[i], refs[2 + i], refs[4].at[i]) for i in range(2)]
    for copy in copies:
        copy.start()
    for copy in copies:
        copy.wait()


def local(source, links, prolongator, coarse_inverse):
    n = lax.axis_size("ta")
    shape = source.shape
    _, sites, rhs, comps = shape
    ks = prolongator.shape[2]
    width, half = sites * rhs, sites * ks
    sums = len(LINK_SUMS)
    vmem = pl.BlockSpec(memory_space=pltpu.VMEM)
    dma = pltpu.SemaphoreType.DMA
    fields = (jax.ShapeDtypeStruct((width, comps), F32),) * 2
    results = pl.pallas_call(
        functools.partial(kernel, n),
        out_shape=(pltpu.VMEM((width, comps), F32),) * 2,
        in_specs=[pl.BlockSpec(memory_space=pl.ANY)] * 4,
        out_specs=(vmem, vmem),
        scratch_shapes=[
            pltpu.VMEM((half, comps), F32),
            pltpu.VMEM(coarse_inverse.shape, F32),
            pltpu.VMEM(links.shape[1:], F32),
            pltpu.VMEM((sites, 2, sums * comps, comps), BF16),
            pltpu.VMEM((15, width, comps), F32),
            pltpu.VMEM((sites, 2 * rhs, comps), BF16),
            pltpu.VMEM((width, comps), F32),
            pltpu.VMEM((7, 2, width, comps), F32),
            pltpu.VMEM((2, half, comps), F32),
            pltpu.VMEM((3, sites, 2 * ks, comps), BF16),
            pltpu.VMEM((sites, 2, 4 * half, comps), BF16),
            pltpu.VMEM((rhs, width), F32),
            pltpu.VMEM((2, rhs, width), F32),
            pltpu.VMEM((width, comps), F32),
            pltpu.VMEM((SWEEPS + 1, ks + 1, width), F32),
            pltpu.VMEM((SWEEPS + 1, 2, n // 2, ks + 1, width), F32),
            pltpu.VMEM((3, SMALL_ROWS, width), F32),
            pltpu.VMEM((3, n, SMALL_ROWS, width), F32),
            pltpu.VMEM((n * half, 2 * width), BF16),
            dma((3,)),
            dma((sites,)),
            dma((7, 2)),
            dma((7, 2, sites)),
            dma((2, 2)),
            dma((2, 2)),
            dma((SWEEPS + 1,)),
            dma((SWEEPS + 1,)),
            dma((SWEEPS + 1,)),
            dma((SWEEPS + 1,)),
            dma((3,)),
            dma((3,)),
        ],
        compiler_params=pltpu.CompilerParams(
            collective_id=0, has_side_effects=True, vmem_limit_bytes=60 * 1024 * 1024
        ),
    )(
        source.reshape(width, comps),
        links,
        prolongator.reshape(half, comps),
        coarse_inverse,
    )
    results = pl.pallas_call(
        hand_over, out_shape=fields, in_specs=[vmem] * 2,
        out_specs=(pl.BlockSpec(memory_space=pl.ANY),) * 2, scratch_shapes=[dma((2,))],
        compiler_params=pltpu.CompilerParams(vmem_limit_bytes=1024 * 1024),
    )(*[pltpu.with_memory_space_constraint(r, pltpu.VMEM) for r in results])
    return tuple(r.reshape(shape) for r in results)


def solution(mesh):
    return jax.shard_map(
        local,
        mesh=mesh,
        in_specs=(
            P(("groups", "ta"), None, None, None),
            P("ta", None, None, None, None),
            P("ta", None, None, None),
            P("ta", None),
        ),
        out_specs=(P(("groups", "ta"), None, None, None), P(("groups", "ta"), None, None, None)),
        check_vma=False,
    )
```

```python
import functools

import jax
import jax.numpy as jnp
from jax import lax
from jax.experimental import pallas as pl
from jax.experimental.pallas import tpu as pltpu
from jax.sharding import PartitionSpec as P

LINK_SUMS = ((0, 3, 4), (5, 6), (7, 8), (1,), (2,))
INNER_SUMS = 3
DAMPING = 0.8
SWEEPS = 3
STEP = 0.8
F32 = jnp.float32
BF16 = jnp.bfloat16
SMALL_ROWS = 2


def dot(a, b):
    return jnp.dot(a, b, preferred_element_type=F32)


def dot_rows(a, b):
    return lax.dot_general(a, b, (((1,), (1,)), ((), ())), preferred_element_type=F32)


def two_parts(a):
    hi = a.astype(BF16)
    return hi, (a - hi.astype(F32)).astype(BF16)


def stacked_parts(a):
    return jnp.concatenate(two_parts(a), axis=0)


def fold(a):
    rows = a.shape[0] // 2
    return a[:rows] + a[rows:]


def kernel(
    n,
    source_ref,
    links_ref,
    prol_ref,
    inverse_ref,
    solution_ref,
    residual_ref,
    prol_in,
    inverse_in,
    raw,
    lcat,
    field,
    parts,
    acc,
    halo,
    prol_halo,
    prol_sites,
    images,
    coarse_out,
    coarse_halo,
    acc_coarse,
    stage,
    gather,
    small_stage,
    small,
    rall,
    input_sem,
    link_sem,
    halo_send,
    halo_recv,
    late_recv,
    near_send,
    near_recv,
    gather_send,
    gather_recv,
    share_send,
    share_recv,
    small_send,
    small_recv,
):
    me = lax.axis_index("ta")
    sites = links_ref.shape[1]
    width, comps = source_ref.shape
    rhs = width // sites
    half = prol_ref.shape[0]
    ks = half // sites
    sums = len(LINK_SUMS)
    right, left = lax.rem(me + 1, n), lax.rem(me + n - 1, n)
    upper = me >= n // 2

    def far_first(start, d):
        return lax.rem(start + jnp.where(upper, d, n - d), n)

    barrier = pltpu.get_barrier_semaphore()

    def greet(d, carry):
        pl.semaphore_signal(barrier, inc=1, device_id={"ta": lax.rem(me + d, n)})
        return carry

    lax.fori_loop(1, n, greet, 0)
    inputs = [
        pltpu.make_async_copy(hbm, vmem, input_sem.at[i])
        for i, (hbm, vmem) in enumerate(
            ((source_ref, field.at[0]), (prol_ref, prol_in), (inverse_ref, inverse_in))
        )
    ]
    inputs[0].start()
    inputs[1].start()
    for s in range(sites):
        pltpu.make_async_copy(links_ref.at[0, s], raw.at[s], link_sem.at[s]).start()
    inputs[2].start()

    lane_site = lax.broadcasted_iota(jnp.int32, (1, width), 1) // rhs

    def over_sites(x):
        shift = rhs
        while shift < width:
            x = x + pltpu.roll(x, shift, 1)
            shift *= 2
        return x

    row_site = lax.broadcasted_iota(jnp.int32, (half, width), 0) // ks
    diagonal = row_site == lax.broadcasted_iota(jnp.int32, (half, width), 1) // rhs

    def rows_of(s, count=rhs):
        return pl.ds(pl.multiple_of(s * count, count), count)

    def dot_parts(a, b):
        p = dot(a, b)
        rows = a.shape[0] // 2
        return p[:rows, :width] + p[:rows, width:] + p[rows:, :width]

    def restrict():
        hi = jnp.concatenate([parts[s, :rhs] for s in range(sites)], axis=0)
        lo = jnp.concatenate([parts[s, rhs:] for s in range(sites)], axis=0)
        full = fold(dot_rows(prol_parts, hi)) + dot_rows(prol_parts[:half], lo)
        full = jnp.where(diagonal, full, 0.0)
        return functools.reduce(jnp.add, [full[s * ks : (s + 1) * ks] for s in range(sites)])

    def products(pairs, rows=1):
        packed = []
        for at in range(0, rows * sites, sites):
            sums_over = []
            for a, b in pairs[at : at + sites]:
                p = a * b
                p = functools.reduce(jnp.add, [p[s * rhs : (s + 1) * rhs] for s in range(sites)])
                sums_over.append(
                    functools.reduce(
                        jnp.add, [p[:, c : c + width] for c in range(0, comps, width)]
                    )
                )
            blank = [jnp.zeros((rhs, width), F32)] * (sites - len(sums_over))
            packed.append(
                jnp.sum(jnp.concatenate(sums_over + blank, axis=0).T, axis=0, keepdims=True)
            )
        return packed[0] if rows == 1 else jnp.concatenate(packed, axis=0)

    def columns(values):
        blank = [jnp.zeros((1, width), F32)] * (-len(values) % 8)
        turned = jnp.concatenate(list(values) + blank, axis=0).T
        return [turned[:, i : i + 1] for i in range(len(values))]

    def halo_arrival(r, side, s):
        return late_recv.at[side] if r == SWEEPS else halo_recv.at[r % 2, side, s]

    def send_site(r, f, s):
        for side, to in ((0, left), (1, right)):
            pltpu.make_async_remote_copy(
                src_ref=field.at[f, rows_of(s)],
                dst_ref=halo.at[r, side, rows_of(s)],
                send_sem=halo_send,
                recv_sem=halo_arrival(r, side, s),
                device_id={"ta": to},
            ).start()

    def send_field(r, f):
        for s in range(sites):
            send_site(r, f, s)

    def near(k, src, dst):
        return [
            pltpu.make_async_remote_copy(
                src_ref=src,
                dst_ref=dst.at[side],
                send_sem=near_send.at[k],
                recv_sem=near_recv.at[k],
                device_id={"ta": to},
            )
            for side, to in ((0, left), (1, right))
        ]

    pending = []

    core, chips = lax.rem(me, 2), n // 2
    partner = me + 1 - 2 * core

    def gather_copy(k, blocks):
        return pltpu.make_async_remote_copy(
            src_ref=gather.at[k, core, blocks],
            dst_ref=gather.at[k, core, blocks],
            send_sem=gather_send,
            recv_sem=gather_recv.at[k],
            device_id={"ta": partner},
        )

    def share_copy(k):
        return pltpu.make_async_remote_copy(
            src_ref=gather.at[k, core],
            dst_ref=gather.at[k, core],
            send_sem=share_send,
            recv_sem=share_recv.at[k],
            device_id={"ta": partner},
        )

    def exchange_large(k, value):
        stage[k] = value
        gather[k, core, me // 2] = value

        def send(to, send_sem, recv_sem):
            pltpu.make_async_remote_copy(
                src_ref=stage.at[k],
                dst_ref=gather.at[k, core, me // 2],
                send_sem=send_sem,
                recv_sem=recv_sem.at[k],
                device_id={"ta": to},
            ).start()

        def one(d, carry):
            send(far_first(me, 2 * d), gather_send, gather_recv)
            if k == SWEEPS:
                send(far_first(partner, 2 * d), share_send, share_recv)
            return carry

        lax.fori_loop(1, chips, one, 0)
        if k == SWEEPS:
            send(partner, share_send, share_recv)

    def share_large(k):
        gather_copy(k, pl.ds(0, chips - 1)).wait_recv()
        if k < SWEEPS:
            share_copy(k).start()

    def exchange_small(k, value):
        small_stage[k] = value
        small[k, me] = value

        def one(d, carry):
            pltpu.make_async_remote_copy(
                src_ref=small_stage.at[k],
                dst_ref=small.at[k, me],
                send_sem=small_send,
                recv_sem=small_recv.at[k],
                device_id={"ta": far_first(me, d)},
            ).start()
            return carry

        lax.fori_loop(1, n, one, 0)
        pending.append(
            pltpu.make_async_remote_copy(
                src_ref=small.at[k, pl.ds(0, n - 1)],
                dst_ref=small.at[k, pl.ds(0, n - 1)],
                send_sem=small_send,
                recv_sem=small_recv.at[k],
                device_id={"ta": right},
            )
        )

    def apply_links(s, vectors, first, last):
        k = slice(first * comps, last * comps)
        return fold(dot(vectors, lcat[s, 0, k]) + dot(vectors, lcat[s, 1, k]))

    def across(s):
        return (s + sites // 2) % sites, s ^ 1

    def load_inner(f):
        for s in range(sites):
            parts[s] = stacked_parts(field[f, s * rhs : (s + 1) * rhs])

    def inner(send=None):
        for s in range(sites):
            if send is not None:
                send_site(*send, s)
            y, z = across(s)
            vectors = jnp.concatenate([parts[s], parts[y], parts[z]], axis=1)
            acc[s * rhs : (s + 1) * rhs] = apply_links(s, vectors, 0, INNER_SUMS)

    def outer(r, f, to, of_field, of_links, send=None, keep=False):
        def arrived(rows, s):
            for side in range(2):
                pltpu.make_async_remote_copy(
                    src_ref=field.at[0, rows],
                    dst_ref=halo.at[r, side, rows],
                    send_sem=halo_send,
                    recv_sem=halo_arrival(r, side, s),
                    device_id={"ta": left},
                ).wait_recv()

        if r == SWEEPS:
            arrived(slice(None), 0)

        def site(s, carry):
            if r != SWEEPS:
                arrived(rows_of(s), s)
            vectors = jnp.concatenate(
                [stacked_parts(halo[r, side, rows_of(s)]) for side in range(2)], axis=1
            )
            links = acc[rows_of(s)] + apply_links(s, vectors, INNER_SUMS, sums)
            new = of_field * field[f, rows_of(s)] + of_links * links
            field[to, rows_of(s)] = new
            if send is not None:
                send_site(send, to, s)
            if keep:
                parts[s] = stacked_parts(new)
            return carry

        lax.fori_loop(0, sites, site, 0)

    def image_of(c):
        last = len(c) - 1
        inside = [(c[i] - c[i - 1]) / STEP for i in range(1, last + 1)]
        return [c[0] / STEP] + inside + [-c[last] / STEP]

    def factor_of(gram, c, d):
        gd = [
            functools.reduce(jnp.add, [gram(i, j) * d[j] for j in range(len(d))])
            for i in range(len(d))
        ]
        across = functools.reduce(jnp.add, [gd[i] * c[i] for i in range(len(c))])
        squared = functools.reduce(jnp.add, [gd[i] * d[i] for i in range(len(d))])
        return DAMPING * across / squared

    def advance(c, x, d, factor):
        x = [x[i] + factor * c[i] if i < len(c) else x[i] for i in range(SWEEPS)]
        return [c[i] - factor * d[i] if i < len(c) else -factor * d[i] for i in range(len(d))], x

    def sweeps(gram, count):
        c = [jnp.ones((1, width), F32)]
        x = [jnp.zeros((1, width), F32)] * SWEEPS
        for _ in range(count):
            d = image_of(c)
            c, x = advance(c, x, d, factor_of(gram, c, d))
        return c, x

    def combine(coefficients, fields):
        return functools.reduce(jnp.add, [a * field[f] for a, f in zip(coefficients, fields)])

    images[...] = jnp.zeros(images.shape, BF16)
    inputs[0].wait()
    pl.semaphore_wait(barrier, n - 1)
    send_field(0, 0)
    load_inner(0)
    inputs[1].wait()
    prol_copies = near(0, prol_in, prol_halo)
    prol_parts = stacked_parts(prol_in[...])

    def prepare(s, carry):
        pltpu.make_async_copy(links_ref.at[0, s], raw.at[s], link_sem.at[s]).wait()
        for at, members in enumerate(LINK_SUMS):
            hi, lo = two_parts(functools.reduce(jnp.add, [raw[s, m] for m in members]).T)
            lcat[s, 0, at * comps : (at + 1) * comps] = hi
            lcat[s, 1, at * comps : (at + 1) * comps] = lo
        return carry

    lax.fori_loop(0, sites, prepare, 0)
    for k in range(SWEEPS + 1):
        value = jnp.concatenate(
            [restrict(), products([(field[k], field[i]) for i in range(k + 1)])], axis=0
        )
        exchange_large(k, value)
        if k == SWEEPS:
            send_field(k, k)
            for copy in prol_copies:
                copy.start()
        inner()
        if k:
            share_large(k - 1)
        if k < SWEEPS:
            outer(k, k, k + 1, 1.0 - STEP, -STEP, k + 1 if k + 1 < SWEEPS else None, True)

    inputs[2].wait()
    inverse_parts = stacked_parts(inverse_in[...])

    def total_of(slots, k, at, rows):
        return jnp.sum(slots.at[k][:, at : at + rows, :], axis=0)

    def unpack(total, i):
        row = total[i // sites : i // sites + 1]
        return over_sites(jnp.where(lane_site == i % sites, row, 0.0))

    def solve_coarse(coefficients):
        def spread(chip, carry):
            for half_chip in range(2):
                r = functools.reduce(
                    jnp.add,
                    [a * gather[k, half_chip, chip, :ks] for k, a in enumerate(coefficients)],
                )
                for s in range(sites):
                    hi, lo = two_parts(jnp.where(lane_site == s, r, 0.0))
                    row = ((2 * chip + half_chip) * sites + s) * ks
                    at = pl.ds(pl.multiple_of(row, ks), ks)
                    rall[at, :width] = hi
                    rall[at, width:] = lo
            return carry

        lax.fori_loop(0, chips, spread, 0, unroll=4)
        return over_sites(dot_parts(inverse_parts, rall[...]))

    grams = {}

    def gram(i, j):
        return grams[max(i, j), min(i, j)]

    def read_grams(k):
        share_copy(k).wait_recv()
        total = functools.reduce(jnp.add, [total_of(gather, (k, c), ks, 1) for c in range(2)])
        grams.update({(k, i): unpack(total, i) for i in range(k + 1)})

    for k in range(SWEEPS):
        read_grams(k)
    c, x = sweeps(gram, SWEEPS - 1)
    d = image_of(c)
    before = solve_coarse(c)
    share_large(SWEEPS)
    read_grams(SWEEPS)
    factor = factor_of(gram, c, d)
    coarse = before - factor * solve_coarse(d)
    coarse_out[...] = jnp.concatenate([coarse, jnp.zeros((width - half, width), F32)], axis=0).T[:rhs]
    coarse_copies = near(1, coarse_out, coarse_halo)
    for copy in coarse_copies:
        copy.start()
    c, x = advance(c, x, d, factor)
    turned = columns(c + x)
    c, x = turned[: len(c)], turned[len(c) :]
    field[7] = combine(c, range(SWEEPS + 1))

    def both_arrived(k, dst):
        pltpu.make_async_remote_copy(
            src_ref=dst,
            dst_ref=dst,
            send_sem=near_send.at[k],
            recv_sem=near_recv.at[k],
            device_id={"ta": left},
        ).wait_recv()

    both_arrived(0, prol_halo)
    for at, block in enumerate((prol_in, prol_halo.at[0], prol_halo.at[1])):
        for s in range(sites):
            prol_sites[at, s] = stacked_parts(block[s * ks : (s + 1) * ks])
    for s in range(sites):
        y, z = across(s)
        terms = ((0, 0, s), (1, 0, y), (2, 0, z), (3, 1, s), (4, 2, s))
        for m, at, site in terms:
            value = apply_links(s, prol_sites[at, site], m, m + 1)
            if m == 0:
                value = value + prol_in[s * ks : (s + 1) * ks]
            row = at * half + site * ks
            images[s, 0, row : row + ks], images[s, 1, row : row + ks] = two_parts(value)

    def vectors_of(block):
        return stacked_parts(block[:, :half])

    def part_of(s, vectors, at):
        k = slice(at * half, (at + 1) * half)
        return fold(dot(vectors, images[s, 0, k]) + dot(vectors, images[s, 1, k]))

    own = vectors_of(coarse_out[...])
    for s in range(sites):
        acc_coarse[s * rhs : (s + 1) * rhs] = part_of(s, own, 0)
    both_arrived(1, coarse_halo)
    around = jnp.concatenate([vectors_of(coarse_halo[side]) for side in range(2)], axis=1)
    for s in range(sites):
        k = slice(half, 3 * half)
        links = fold(dot(around, images[s, 0, k]) + dot(around, images[s, 1, k]))
        new = acc_coarse[s * rhs : (s + 1) * rhs] + links
        field[6, s * rhs : (s + 1) * rhs] = new
        send_site(4, 6, s)
        parts[s] = stacked_parts(new)
    exchange_small(0, products([(field[6], field[7]), (field[6], field[6])], SMALL_ROWS))
    outer(SWEEPS, SWEEPS, SWEEPS + 1, 1.0 - STEP, -STEP)
    inner()
    field[8] = combine(c, range(1, SWEEPS + 2))
    field[9] = combine(x, range(SWEEPS))
    spread_hi, spread_lo = two_parts(jnp.where(diagonal, coarse, 0.0).T)
    field[5] = (
        dot(spread_hi, prol_parts[:half])
        + dot(spread_lo, prol_parts[:half])
        + dot(spread_hi, prol_parts[half:])
    )
    outer(4, 6, 14, 1.0 - STEP, -STEP)
    pending[-1].wait_recv()
    pair = total_of(small, 0, 0, SMALL_ROWS)
    g = columns([unpack(pair, 0) / unpack(pair, 1)])[0]

    for s in range(sites):
        at = slice(s * rhs, (s + 1) * rhs)
        new = field[8, at] - g[at] * field[14, at]
        field[11, at] = new
        parts[s] = stacked_parts(new)
    inner((5, 11))
    field[10] = field[7] - g * field[6]
    field[9] = field[9] + g * field[5]
    outer(5, 11, 12, 1.0 - STEP, -STEP, 6, True)
    early = [(i, j) for i in range(3) for j in range(i + 1)]
    late = [(3, j) for j in range(4)]
    exchange_small(1, products([(field[10 + i], field[10 + j]) for i, j in early], SMALL_ROWS))
    inner()
    outer(6, 12, 13, 1.0 - STEP, -STEP)
    exchange_small(2, products([(field[10 + i], field[10 + j]) for i, j in late], SMALL_ROWS))
    def all_sent(ref, sem):
        pltpu.make_async_remote_copy(
            src_ref=ref, dst_ref=ref, send_sem=sem, recv_sem=late_recv.at[0], device_id={"ta": left}
        ).wait_send()

    all_sent(halo, halo_send)
    all_sent(gather.at[:, 0, pl.ds(0, chips - 1)], gather_send)
    all_sent(gather.at[:, 0], share_send)
    all_sent(prol_halo, near_send.at[0])
    all_sent(coarse_halo, near_send.at[1])
    pending[-2].wait_recv()
    total = total_of(small, 1, 0, SMALL_ROWS)
    grams = {pair: unpack(total, early.index(pair)) for pair in early}
    c, x = sweeps(gram, SWEEPS - 1)
    d = image_of(c)
    pending[-1].wait_recv()
    total = total_of(small, 2, 0, SMALL_ROWS)
    grams.update({pair: unpack(total, late.index(pair)) for pair in late})
    c, x = advance(c, x, d, factor_of(gram, c, d))
    turned = columns(c + x)
    residual_ref[...] = combine(turned[: len(c)], range(10, 14))
    solution_ref[...] = field[9] + combine(turned[len(c) :], range(10, 13))
    all_sent(small.at[:, pl.ds(0, n - 1)], small_send)


def hand_over(*refs):
    copies = [pltpu.make_async_copy(refs[i], refs[2 + i], refs[4].at[i]) for i in range(2)]
    for copy in copies:
        copy.start()
    for copy in copies:
        copy.wait()


def local(source, links, prolongator, coarse_inverse):
    n = lax.axis_size("ta")
    shape = source.shape
    _, sites, rhs, comps = shape
    ks = prolongator.shape[2]
    width, half = sites * rhs, sites * ks
    sums = len(LINK_SUMS)
    vmem = pl.BlockSpec(memory_space=pltpu.VMEM)
    dma = pltpu.SemaphoreType.DMA
    fields = (jax.ShapeDtypeStruct((width, comps), F32),) * 2
    results = pl.pallas_call(
        functools.partial(kernel, n),
        out_shape=(pltpu.VMEM((width, comps), F32),) * 2,
        in_specs=[pl.BlockSpec(memory_space=pl.ANY)] * 4,
        out_specs=(vmem, vmem),
        scratch_shapes=[
            pltpu.VMEM((half, comps), F32),
            pltpu.VMEM(coarse_inverse.shape, F32),
            pltpu.VMEM(links.shape[1:], F32),
            pltpu.VMEM((sites, 2, sums * comps, comps), BF16),
            pltpu.VMEM((15, width, comps), F32),
            pltpu.VMEM((sites, 2 * rhs, comps), BF16),
            pltpu.VMEM((width, comps), F32),
            pltpu.VMEM((7, 2, width, comps), F32),
            pltpu.VMEM((2, half, comps), F32),
            pltpu.VMEM((3, sites, 2 * ks, comps), BF16),
            pltpu.VMEM((sites, 2, 4 * half, comps), BF16),
            pltpu.VMEM((rhs, width), F32),
            pltpu.VMEM((2, rhs, width), F32),
            pltpu.VMEM((width, comps), F32),
            pltpu.VMEM((SWEEPS + 1, ks + 1, width), F32),
            pltpu.VMEM((SWEEPS + 1, 2, n // 2, ks + 1, width), F32),
            pltpu.VMEM((3, SMALL_ROWS, width), F32),
            pltpu.VMEM((3, n, SMALL_ROWS, width), F32),
            pltpu.VMEM((n * half, 2 * width), BF16),
            dma((3,)),
            dma((sites,)),
            dma,
            dma((2, 2, sites)),
            dma((2,)),
            dma((2,)),
            dma((2,)),
            dma,
            dma((SWEEPS + 1,)),
            dma,
            dma((SWEEPS + 1,)),
            dma,
            dma((3,)),
        ],
        compiler_params=pltpu.CompilerParams(
            collective_id=0, has_side_effects=True, vmem_limit_bytes=60 * 1024 * 1024
        ),
    )(
        source.reshape(width, comps),
        links,
        prolongator.reshape(half, comps),
        coarse_inverse,
    )
    results = pl.pallas_call(
        hand_over, out_shape=fields, in_specs=[vmem] * 2,
        out_specs=(pl.BlockSpec(memory_space=pl.ANY),) * 2, scratch_shapes=[dma((2,))],
        compiler_params=pltpu.CompilerParams(vmem_limit_bytes=1024 * 1024),
    )(*[pltpu.with_memory_space_constraint(r, pltpu.VMEM) for r in results])
    return tuple(r.reshape(shape) for r in results)


def solution(mesh):
    return jax.shard_map(
        local,
        mesh=mesh,
        in_specs=(
            P(("groups", "ta"), None, None, None),
            P("ta", None, None, None, None),
            P("ta", None, None, None),
            P("ta", None),
        ),
        out_specs=(P(("groups", "ta"), None, None, None), P(("groups", "ta"), None, None, None)),
        check_vma=False,
    )
```

```python
import functools

import jax
import jax.numpy as jnp
from jax import lax
from jax.experimental import pallas as pl
from jax.experimental.pallas import tpu as pltpu
from jax.sharding import PartitionSpec as P

LINK_SUMS = ((0, 3, 4), (5, 6), (7, 8), (1,), (2,))
INNER_SUMS = 3
DAMPING = 0.8
SWEEPS = 3
STEP = 0.8
F32 = jnp.float32
BF16 = jnp.bfloat16
SMALL_ROWS = 2


def dot(a, b):
    return jnp.dot(a, b, preferred_element_type=F32)


def dot_rows(a, b):
    return lax.dot_general(a, b, (((1,), (1,)), ((), ())), preferred_element_type=F32)


def two_parts(a):
    hi = a.astype(BF16)
    return hi, (a - hi.astype(F32)).astype(BF16)


def stacked_parts(a):
    return jnp.concatenate(two_parts(a), axis=0)


def fold(a):
    rows = a.shape[0] // 2
    return a[:rows] + a[rows:]


def kernel(
    n,
    source_ref,
    links_ref,
    prol_ref,
    inverse_ref,
    solution_ref,
    residual_ref,
    prol_in,
    inverse_in,
    raw,
    lcat,
    field,
    parts,
    acc,
    halo,
    prol_halo,
    prol_sites,
    images,
    coarse_out,
    coarse_halo,
    acc_coarse,
    stage,
    gather,
    small_stage,
    small,
    rall,
    input_sem,
    link_sem,
    halo_send,
    halo_recv,
    late_recv,
    near_send,
    near_recv,
    gather_send,
    gather_recv,
    share_send,
    share_recv,
    small_send,
    small_recv,
):
    me = lax.axis_index("ta")
    sites = links_ref.shape[1]
    width, comps = source_ref.shape
    rhs = width // sites
    half = prol_ref.shape[0]
    ks = half // sites
    sums = len(LINK_SUMS)
    right, left = lax.rem(me + 1, n), lax.rem(me + n - 1, n)
    upper = me >= n // 2

    def far_first(start, d):
        return lax.rem(start + jnp.where(upper, d, n - d), n)

    barrier = pltpu.get_barrier_semaphore()

    def greet(d, carry):
        pl.semaphore_signal(barrier, inc=1, device_id={"ta": lax.rem(me + d, n)})
        return carry

    lax.fori_loop(1, n, greet, 0)
    inputs = [
        pltpu.make_async_copy(hbm, vmem, input_sem.at[i])
        for i, (hbm, vmem) in enumerate(
            ((source_ref, field.at[0]), (prol_ref, prol_in), (inverse_ref, inverse_in))
        )
    ]
    inputs[0].start()
    inputs[1].start()
    for s in range(sites):
        pltpu.make_async_copy(links_ref.at[0, s], raw.at[s], link_sem.at[s]).start()
    inputs[2].start()

    lane_site = lax.broadcasted_iota(jnp.int32, (1, width), 1) // rhs

    def over_sites(x):
        shift = rhs
        while shift < width:
            x = x + pltpu.roll(x, shift, 1)
            shift *= 2
        return x

    row_site = lax.broadcasted_iota(jnp.int32, (half, width), 0) // ks
    diagonal = row_site == lax.broadcasted_iota(jnp.int32, (half, width), 1) // rhs

    def rows_of(s, count=rhs):
        return pl.ds(pl.multiple_of(s * count, count), count)

    def dot_parts(a, b):
        p = dot(a, b)
        rows = a.shape[0] // 2
        return p[:rows, :width] + p[:rows, width:] + p[rows:, :width]

    def restrict():
        hi = jnp.concatenate([parts[s, :rhs] for s in range(sites)], axis=0)
        lo = jnp.concatenate([parts[s, rhs:] for s in range(sites)], axis=0)
        full = fold(dot_rows(prol_parts, hi)) + dot_rows(prol_parts[:half], lo)
        full = jnp.where(diagonal, full, 0.0)
        return functools.reduce(jnp.add, [full[s * ks : (s + 1) * ks] for s in range(sites)])

    def products(pairs, rows=1):
        packed = []
        for at in range(0, rows * sites, sites):
            sums_over = []
            for a, b in pairs[at : at + sites]:
                p = a * b
                p = functools.reduce(jnp.add, [p[s * rhs : (s + 1) * rhs] for s in range(sites)])
                sums_over.append(
                    functools.reduce(
                        jnp.add, [p[:, c : c + width] for c in range(0, comps, width)]
                    )
                )
            blank = [jnp.zeros((rhs, width), F32)] * (sites - len(sums_over))
            packed.append(
                jnp.sum(jnp.concatenate(sums_over + blank, axis=0).T, axis=0, keepdims=True)
            )
        return packed[0] if rows == 1 else jnp.concatenate(packed, axis=0)

    def columns(values):
        blank = [jnp.zeros((1, width), F32)] * (-len(values) % 8)
        turned = jnp.concatenate(list(values) + blank, axis=0).T
        return [turned[:, i : i + 1] for i in range(len(values))]

    def halo_arrival(r, side, s):
        return late_recv.at[side] if r == SWEEPS else halo_recv.at[r % 2, side, s]

    def send_site(r, f, s):
        for side, to in ((0, left), (1, right)):
            pltpu.make_async_remote_copy(
                src_ref=field.at[f, rows_of(s)],
                dst_ref=halo.at[r, side, rows_of(s)],
                send_sem=halo_send,
                recv_sem=halo_arrival(r, side, s),
                device_id={"ta": to},
            ).start()

    def send_field(r, f):
        for s in range(sites):
            send_site(r, f, s)

    def near(k, src, dst):
        return [
            pltpu.make_async_remote_copy(
                src_ref=src,
                dst_ref=dst.at[side],
                send_sem=near_send.at[k],
                recv_sem=near_recv.at[k],
                device_id={"ta": to},
            )
            for side, to in ((0, left), (1, right))
        ]

    pending = []

    core, chips = lax.rem(me, 2), n // 2
    partner = me + 1 - 2 * core

    def gather_copy(k, blocks):
        return pltpu.make_async_remote_copy(
            src_ref=gather.at[k, core, blocks],
            dst_ref=gather.at[k, core, blocks],
            send_sem=gather_send,
            recv_sem=gather_recv.at[k],
            device_id={"ta": partner},
        )

    def share_copy(k):
        return pltpu.make_async_remote_copy(
            src_ref=gather.at[k, core],
            dst_ref=gather.at[k, core],
            send_sem=share_send,
            recv_sem=share_recv.at[k],
            device_id={"ta": partner},
        )

    def exchange_large(k, value):
        stage[k] = value
        gather[k, core, me // 2] = value

        def send(to, send_sem, recv_sem):
            pltpu.make_async_remote_copy(
                src_ref=stage.at[k],
                dst_ref=gather.at[k, core, me // 2],
                send_sem=send_sem,
                recv_sem=recv_sem.at[k],
                device_id={"ta": to},
            ).start()

        def one(d, carry):
            send(far_first(me, 2 * d), gather_send, gather_recv)
            if k == SWEEPS:
                send(far_first(partner, 2 * d), share_send, share_recv)
            return carry

        lax.fori_loop(1, chips, one, 0)
        if k == SWEEPS:
            send(partner, share_send, share_recv)

    def share_large(k):
        gather_copy(k, pl.ds(0, chips - 1)).wait_recv()
        if k < SWEEPS:
            share_copy(k).start()

    def exchange_small(k, value):
        small_stage[k] = value
        small[k, me] = value

        def one(d, carry):
            pltpu.make_async_remote_copy(
                src_ref=small_stage.at[k],
                dst_ref=small.at[k, me],
                send_sem=small_send,
                recv_sem=small_recv.at[k],
                device_id={"ta": far_first(me, d)},
            ).start()
            return carry

        lax.fori_loop(1, n, one, 0)
        pending.append(
            pltpu.make_async_remote_copy(
                src_ref=small.at[k, pl.ds(0, n - 1)],
                dst_ref=small.at[k, pl.ds(0, n - 1)],
                send_sem=small_send,
                recv_sem=small_recv.at[k],
                device_id={"ta": right},
            )
        )

    def apply_links(s, vectors, first, last):
        k = slice(first * comps, last * comps)
        return fold(dot(vectors, lcat[s, 0, k]) + dot(vectors, lcat[s, 1, k]))

    def across(s):
        return (s + sites // 2) % sites, s ^ 1

    def load_inner(f):
        for s in range(sites):
            parts[s] = stacked_parts(field[f, s * rhs : (s + 1) * rhs])

    def inner(send=None):
        for s in range(sites):
            if send is not None:
                send_site(*send, s)
            y, z = across(s)
            vectors = jnp.concatenate([parts[s], parts[y], parts[z]], axis=1)
            acc[s * rhs : (s + 1) * rhs] = apply_links(s, vectors, 0, INNER_SUMS)

    def outer(r, f, to, of_field, of_links, send=None, keep=False):
        def arrived(rows, s):
            for side in range(2):
                pltpu.make_async_remote_copy(
                    src_ref=field.at[0, rows],
                    dst_ref=halo.at[r, side, rows],
                    send_sem=halo_send,
                    recv_sem=halo_arrival(r, side, s),
                    device_id={"ta": left},
                ).wait_recv()

        if r == SWEEPS:
            arrived(slice(None), 0)

        def site(s, carry):
            if r != SWEEPS:
                arrived(rows_of(s), s)
            vectors = jnp.concatenate(
                [stacked_parts(halo[r, side, rows_of(s)]) for side in range(2)], axis=1
            )
            links = acc[rows_of(s)] + apply_links(s, vectors, INNER_SUMS, sums)
            new = of_field * field[f, rows_of(s)] + of_links * links
            field[to, rows_of(s)] = new
            if send is not None:
                send_site(send, to, s)
            if keep:
                parts[s] = stacked_parts(new)
            return carry

        lax.fori_loop(0, sites, site, 0)

    def image_of(c):
        last = len(c) - 1
        inside = [(c[i] - c[i - 1]) / STEP for i in range(1, last + 1)]
        return [c[0] / STEP] + inside + [-c[last] / STEP]

    def factor_of(gram, c, d):
        gd = [
            functools.reduce(jnp.add, [gram(i, j) * d[j] for j in range(len(d))])
            for i in range(len(d))
        ]
        across = functools.reduce(jnp.add, [gd[i] * c[i] for i in range(len(c))])
        squared = functools.reduce(jnp.add, [gd[i] * d[i] for i in range(len(d))])
        return DAMPING * across / squared

    def advance(c, x, d, factor):
        x = [x[i] + factor * c[i] if i < len(c) else x[i] for i in range(SWEEPS)]
        return [c[i] - factor * d[i] if i < len(c) else -factor * d[i] for i in range(len(d))], x

    def sweeps(gram, count):
        c = [jnp.ones((1, width), F32)]
        x = [jnp.zeros((1, width), F32)] * SWEEPS
        for _ in range(count):
            d = image_of(c)
            c, x = advance(c, x, d, factor_of(gram, c, d))
        return c, x

    def combine(coefficients, fields):
        return functools.reduce(jnp.add, [a * field[f] for a, f in zip(coefficients, fields)])

    images[...] = jnp.zeros(images.shape, BF16)
    inputs[0].wait()
    pl.semaphore_wait(barrier, n - 1)
    send_field(0, 0)
    load_inner(0)
    inputs[1].wait()
    prol_copies = near(0, prol_in, prol_halo)
    prol_parts = stacked_parts(prol_in[...])

    def prepare(s, carry):
        pltpu.make_async_copy(links_ref.at[0, s], raw.at[s], link_sem.at[s]).wait()
        for at, members in enumerate(LINK_SUMS):
            hi, lo = two_parts(functools.reduce(jnp.add, [raw[s, m] for m in members]).T)
            lcat[s, 0, at * comps : (at + 1) * comps] = hi
            lcat[s, 1, at * comps : (at + 1) * comps] = lo
        return carry

    lax.fori_loop(0, sites, prepare, 0)
    for k in range(SWEEPS + 1):
        value = jnp.concatenate(
            [restrict(), products([(field[k], field[i]) for i in range(k + 1)])], axis=0
        )
        exchange_large(k, value)
        if k == SWEEPS:
            send_field(k, k)
            for copy in prol_copies:
                copy.start()
        inner()
        if k:
            share_large(k - 1)
        if k < SWEEPS:
            outer(k, k, k + 1, 1.0 - STEP, -STEP, k + 1 if k + 1 < SWEEPS else None, True)

    inputs[2].wait()
    inverse_parts = stacked_parts(inverse_in[...])

    def total_of(slots, k, at, rows):
        return jnp.sum(slots.at[k][:, at : at + rows, :], axis=0)

    def unpack(total, i):
        row = total[i // sites : i // sites + 1]
        return over_sites(jnp.where(lane_site == i % sites, row, 0.0))

    def solve_coarse(coefficients):
        def spread(chip, carry):
            for half_chip in range(2):
                r = functools.reduce(
                    jnp.add,
                    [a * gather[k, half_chip, chip, :ks] for k, a in enumerate(coefficients)],
                )
                for s in range(sites):
                    hi, lo = two_parts(jnp.where(lane_site == s, r, 0.0))
                    row = ((2 * chip + half_chip) * sites + s) * ks
                    at = pl.ds(pl.multiple_of(row, ks), ks)
                    rall[at, :width] = hi
                    rall[at, width:] = lo
            return carry

        lax.fori_loop(0, chips, spread, 0, unroll=4)
        return over_sites(dot_parts(inverse_parts, rall[...]))

    grams = {}

    def gram(i, j):
        return grams[max(i, j), min(i, j)]

    def read_grams(k):
        share_copy(k).wait_recv()
        total = functools.reduce(jnp.add, [total_of(gather, (k, c), ks, 1) for c in range(2)])
        grams.update({(k, i): unpack(total, i) for i in range(k + 1)})

    for k in range(SWEEPS):
        read_grams(k)
    c, x = sweeps(gram, SWEEPS - 1)
    d = image_of(c)
    before = solve_coarse(c)
    share_large(SWEEPS)
    read_grams(SWEEPS)
    factor = factor_of(gram, c, d)
    coarse = before - factor * solve_coarse(d)
    coarse_out[...] = jnp.concatenate([coarse, jnp.zeros((width - half, width), F32)], axis=0).T[:rhs]
    coarse_copies = near(1, coarse_out, coarse_halo)
    for copy in coarse_copies:
        copy.start()
    c, x = advance(c, x, d, factor)
    turned = columns(c + x)
    c, x = turned[: len(c)], turned[len(c) :]
    field[7] = combine(c, range(SWEEPS + 1))

    def both_arrived(k, dst):
        pltpu.make_async_remote_copy(
            src_ref=dst,
            dst_ref=dst,
            send_sem=near_send.at[k],
            recv_sem=near_recv.at[k],
            device_id={"ta": left},
        ).wait_recv()

    both_arrived(0, prol_halo)
    for at, block in enumerate((prol_in, prol_halo.at[0], prol_halo.at[1])):
        for s in range(sites):
            prol_sites[at, s] = stacked_parts(block[s * ks : (s + 1) * ks])
    for s in range(sites):
        y, z = across(s)
        terms = ((0, 0, s), (1, 0, y), (2, 0, z), (3, 1, s), (4, 2, s))
        for m, at, site in terms:
            value = apply_links(s, prol_sites[at, site], m, m + 1)
            if m == 0:
                value = value + prol_in[s * ks : (s + 1) * ks]
            row = at * half + site * ks
            images[s, 0, row : row + ks], images[s, 1, row : row + ks] = two_parts(value)

    def vectors_of(block):
        return stacked_parts(block[:, :half])

    def part_of(s, vectors, at):
        k = slice(at * half, (at + 1) * half)
        return fold(dot(vectors, images[s, 0, k]) + dot(vectors, images[s, 1, k]))

    own = vectors_of(coarse_out[...])
    for s in range(sites):
        acc_coarse[s * rhs : (s + 1) * rhs] = part_of(s, own, 0)
    both_arrived(1, coarse_halo)
    around = jnp.concatenate([vectors_of(coarse_halo[side]) for side in range(2)], axis=1)
    for s in range(sites):
        k = slice(half, 3 * half)
        links = fold(dot(around, images[s, 0, k]) + dot(around, images[s, 1, k]))
        new = acc_coarse[s * rhs : (s + 1) * rhs] + links
        field[6, s * rhs : (s + 1) * rhs] = new
        if s < sites // 2:
            send_site(4, 6, s)
    exchange_small(0, products([(field[6], field[7]), (field[6], field[6])], SMALL_ROWS))
    for s in range(sites // 2, sites):
        send_site(4, 6, s)
    load_inner(6)
    outer(SWEEPS, SWEEPS, SWEEPS + 1, 1.0 - STEP, -STEP)
    inner()
    field[8] = combine(c, range(1, SWEEPS + 2))
    field[9] = combine(x, range(SWEEPS))
    spread_hi, spread_lo = two_parts(jnp.where(diagonal, coarse, 0.0).T)
    field[5] = (
        dot(spread_hi, prol_parts[:half])
        + dot(spread_lo, prol_parts[:half])
        + dot(spread_hi, prol_parts[half:])
    )
    outer(4, 6, 14, 1.0 - STEP, -STEP)
    pending[-1].wait_recv()
    pair = total_of(small, 0, 0, SMALL_ROWS)
    g = columns([unpack(pair, 0) / unpack(pair, 1)])[0]

    for s in range(sites):
        at = slice(s * rhs, (s + 1) * rhs)
        new = field[8, at] - g[at] * field[14, at]
        field[11, at] = new
        parts[s] = stacked_parts(new)
    inner((5, 11))
    field[10] = field[7] - g * field[6]
    field[9] = field[9] + g * field[5]
    outer(5, 11, 12, 1.0 - STEP, -STEP, 6, True)
    early = [(i, j) for i in range(3) for j in range(i + 1)]
    late = [(3, j) for j in range(4)]
    exchange_small(1, products([(field[10 + i], field[10 + j]) for i, j in early], SMALL_ROWS))
    inner()
    outer(6, 12, 13, 1.0 - STEP, -STEP)
    exchange_small(2, products([(field[10 + i], field[10 + j]) for i, j in late], SMALL_ROWS))
    def all_sent(ref, sem):
        pltpu.make_async_remote_copy(
            src_ref=ref, dst_ref=ref, send_sem=sem, recv_sem=late_recv.at[0], device_id={"ta": left}
        ).wait_send()

    all_sent(halo, halo_send)
    all_sent(gather.at[:, 0, pl.ds(0, chips - 1)], gather_send)
    all_sent(gather.at[:, 0], share_send)
    all_sent(prol_halo, near_send.at[0])
    all_sent(coarse_halo, near_send.at[1])
    pending[-2].wait_recv()
    total = total_of(small, 1, 0, SMALL_ROWS)
    grams = {pair: unpack(total, early.index(pair)) for pair in early}
    c, x = sweeps(gram, SWEEPS - 1)
    d = image_of(c)
    pending[-1].wait_recv()
    total = total_of(small, 2, 0, SMALL_ROWS)
    grams.update({pair: unpack(total, late.index(pair)) for pair in late})
    c, x = advance(c, x, d, factor_of(gram, c, d))
    turned = columns(c + x)
    residual_ref[...] = combine(turned[: len(c)], range(10, 14))
    solution_ref[...] = field[9] + combine(turned[len(c) :], range(10, 13))
    all_sent(small.at[:, pl.ds(0, n - 1)], small_send)


def hand_over(*refs):
    copies = [pltpu.make_async_copy(refs[i], refs[2 + i], refs[4].at[i]) for i in range(2)]
    for copy in copies:
        copy.start()
    for copy in copies:
        copy.wait()


def local(source, links, prolongator, coarse_inverse):
    n = lax.axis_size("ta")
    shape = source.shape
    _, sites, rhs, comps = shape
    ks = prolongator.shape[2]
    width, half = sites * rhs, sites * ks
    sums = len(LINK_SUMS)
    vmem = pl.BlockSpec(memory_space=pltpu.VMEM)
    dma = pltpu.SemaphoreType.DMA
    fields = (jax.ShapeDtypeStruct((width, comps), F32),) * 2
    results = pl.pallas_call(
        functools.partial(kernel, n),
        out_shape=(pltpu.VMEM((width, comps), F32),) * 2,
        in_specs=[pl.BlockSpec(memory_space=pl.ANY)] * 4,
        out_specs=(vmem, vmem),
        scratch_shapes=[
            pltpu.VMEM((half, comps), F32),
            pltpu.VMEM(coarse_inverse.shape, F32),
            pltpu.VMEM(links.shape[1:], F32),
            pltpu.VMEM((sites, 2, sums * comps, comps), BF16),
            pltpu.VMEM((15, width, comps), F32),
            pltpu.VMEM((sites, 2 * rhs, comps), BF16),
            pltpu.VMEM((width, comps), F32),
            pltpu.VMEM((7, 2, width, comps), F32),
            pltpu.VMEM((2, half, comps), F32),
            pltpu.VMEM((3, sites, 2 * ks, comps), BF16),
            pltpu.VMEM((sites, 2, 4 * half, comps), BF16),
            pltpu.VMEM((rhs, width), F32),
            pltpu.VMEM((2, rhs, width), F32),
            pltpu.VMEM((width, comps), F32),
            pltpu.VMEM((SWEEPS + 1, ks + 1, width), F32),
            pltpu.VMEM((SWEEPS + 1, 2, n // 2, ks + 1, width), F32),
            pltpu.VMEM((3, SMALL_ROWS, width), F32),
            pltpu.VMEM((3, n, SMALL_ROWS, width), F32),
            pltpu.VMEM((n * half, 2 * width), BF16),
            dma((3,)),
            dma((sites,)),
            dma,
            dma((2, 2, sites)),
            dma((2,)),
            dma((2,)),
            dma((2,)),
            dma,
            dma((SWEEPS + 1,)),
            dma,
            dma((SWEEPS + 1,)),
            dma,
            dma((3,)),
        ],
        compiler_params=pltpu.CompilerParams(
            collective_id=0, has_side_effects=True, vmem_limit_bytes=60 * 1024 * 1024
        ),
    )(
        source.reshape(width, comps),
        links,
        prolongator.reshape(half, comps),
        coarse_inverse,
    )
    results = pl.pallas_call(
        hand_over, out_shape=fields, in_specs=[vmem] * 2,
        out_specs=(pl.BlockSpec(memory_space=pl.ANY),) * 2, scratch_shapes=[dma((2,))],
        compiler_params=pltpu.CompilerParams(vmem_limit_bytes=1024 * 1024),
    )(*[pltpu.with_memory_space_constraint(r, pltpu.VMEM) for r in results])
    return tuple(r.reshape(shape) for r in results)


def solution(mesh):
    return jax.shard_map(
        local,
        mesh=mesh,
        in_specs=(
            P(("groups", "ta"), None, None, None),
            P("ta", None, None, None, None),
            P("ta", None, None, None),
            P("ta", None),
        ),
        out_specs=(P(("groups", "ta"), None, None, None), P(("groups", "ta"), None, None, None)),
        check_vma=False,
    )
```

```python
import functools

import jax
import jax.numpy as jnp
from jax import lax
from jax.experimental import pallas as pl
from jax.experimental.pallas import tpu as pltpu
from jax.sharding import PartitionSpec as P

LINK_SUMS = ((0, 3, 4), (5, 6), (7, 8), (1,), (2,))
INNER_SUMS = 3
DAMPING = 0.8
SWEEPS = 3
STEP = 0.8
F32 = jnp.float32
BF16 = jnp.bfloat16
SMALL_ROWS = 2


def dot(a, b):
    return jnp.dot(a, b, preferred_element_type=F32)


def dot_rows(a, b):
    return lax.dot_general(a, b, (((1,), (1,)), ((), ())), preferred_element_type=F32)


def two_parts(a):
    hi = a.astype(BF16)
    return hi, (a - hi.astype(F32)).astype(BF16)


def stacked_parts(a):
    return jnp.concatenate(two_parts(a), axis=0)


def fold(a):
    rows = a.shape[0] // 2
    return a[:rows] + a[rows:]


def kernel(
    n,
    source_ref,
    links_ref,
    prol_ref,
    inverse_ref,
    solution_ref,
    residual_ref,
    prol_in,
    inverse_in,
    raw,
    lcat,
    field,
    parts,
    acc,
    halo,
    prol_halo,
    prol_sites,
    images,
    coarse_out,
    coarse_halo,
    acc_coarse,
    stage,
    gather,
    small_stage,
    small,
    rall,
    input_sem,
    link_sem,
    halo_send,
    halo_recv,
    late_recv,
    near_send,
    near_recv,
    gather_send,
    gather_recv,
    share_send,
    share_recv,
    small_send,
    small_recv,
):
    me = lax.axis_index("ta")
    sites = links_ref.shape[1]
    width, comps = source_ref.shape
    rhs = width // sites
    half = prol_ref.shape[0]
    ks = half // sites
    sums = len(LINK_SUMS)
    right, left = lax.rem(me + 1, n), lax.rem(me + n - 1, n)
    upper = me >= n // 2

    def far_first(start, d):
        return lax.rem(start + jnp.where(upper, d, n - d), n)

    barrier = pltpu.get_barrier_semaphore()

    def greet(d, carry):
        pl.semaphore_signal(barrier, inc=1, device_id={"ta": lax.rem(me + d, n)})
        return carry

    lax.fori_loop(1, n, greet, 0)
    inputs = [
        pltpu.make_async_copy(hbm, vmem, input_sem.at[i])
        for i, (hbm, vmem) in enumerate(
            ((source_ref, field.at[0]), (prol_ref, prol_in), (inverse_ref, inverse_in))
        )
    ]
    inputs[0].start()
    inputs[1].start()
    for s in range(sites):
        pltpu.make_async_copy(links_ref.at[0, s], raw.at[s], link_sem.at[s]).start()
    inputs[2].start()

    lane_site = lax.broadcasted_iota(jnp.int32, (1, width), 1) // rhs

    def over_sites(x):
        shift = rhs
        while shift < width:
            x = x + pltpu.roll(x, shift, 1)
            shift *= 2
        return x

    row_site = lax.broadcasted_iota(jnp.int32, (half, width), 0) // ks
    diagonal = row_site == lax.broadcasted_iota(jnp.int32, (half, width), 1) // rhs

    def rows_of(s, count=rhs):
        return pl.ds(pl.multiple_of(s * count, count), count)

    def dot_parts(a, b):
        p = dot(a, b)
        rows = a.shape[0] // 2
        return p[:rows, :width] + p[:rows, width:] + p[rows:, :width]

    def restrict():
        hi = jnp.concatenate([parts[s, :rhs] for s in range(sites)], axis=0)
        lo = jnp.concatenate([parts[s, rhs:] for s in range(sites)], axis=0)
        full = fold(dot_rows(prol_parts, hi)) + dot_rows(prol_parts[:half], lo)
        full = jnp.where(diagonal, full, 0.0)
        return functools.reduce(jnp.add, [full[s * ks : (s + 1) * ks] for s in range(sites)])

    def products(pairs, rows=1):
        packed = []
        for at in range(0, rows * sites, sites):
            sums_over = []
            for a, b in pairs[at : at + sites]:
                p = a * b
                p = functools.reduce(jnp.add, [p[s * rhs : (s + 1) * rhs] for s in range(sites)])
                sums_over.append(
                    functools.reduce(
                        jnp.add, [p[:, c : c + width] for c in range(0, comps, width)]
                    )
                )
            blank = [jnp.zeros((rhs, width), F32)] * (sites - len(sums_over))
            packed.append(
                jnp.sum(jnp.concatenate(sums_over + blank, axis=0).T, axis=0, keepdims=True)
            )
        return packed[0] if rows == 1 else jnp.concatenate(packed, axis=0)

    def columns(values):
        blank = [jnp.zeros((1, width), F32)] * (-len(values) % 8)
        turned = jnp.concatenate(list(values) + blank, axis=0).T
        return [turned[:, i : i + 1] for i in range(len(values))]

    def halo_arrival(r, s):
        return late_recv if r == SWEEPS else halo_recv.at[r % 2, s]

    def send_site(r, f, s):
        for side, to in ((0, left), (1, right)):
            pltpu.make_async_remote_copy(
                src_ref=field.at[f, rows_of(s)],
                dst_ref=halo.at[r, side, rows_of(s)],
                send_sem=halo_send,
                recv_sem=halo_arrival(r, s),
                device_id={"ta": to},
            ).start()

    def send_field(r, f):
        for s in range(sites):
            send_site(r, f, s)

    def near(k, src, dst):
        return [
            pltpu.make_async_remote_copy(
                src_ref=src,
                dst_ref=dst.at[side],
                send_sem=near_send.at[k],
                recv_sem=near_recv.at[k],
                device_id={"ta": to},
            )
            for side, to in ((0, left), (1, right))
        ]

    pending = []

    core, chips = lax.rem(me, 2), n // 2
    partner = me + 1 - 2 * core

    def gather_copy(k, blocks):
        return pltpu.make_async_remote_copy(
            src_ref=gather.at[k, core, blocks],
            dst_ref=gather.at[k, core, blocks],
            send_sem=gather_send,
            recv_sem=gather_recv.at[k],
            device_id={"ta": partner},
        )

    def share_copy(k):
        return pltpu.make_async_remote_copy(
            src_ref=gather.at[k, core],
            dst_ref=gather.at[k, core],
            send_sem=share_send,
            recv_sem=share_recv.at[k],
            device_id={"ta": partner},
        )

    def exchange_large(k, value):
        stage[k] = value
        gather[k, core, me // 2] = value

        def send(to, send_sem, recv_sem):
            pltpu.make_async_remote_copy(
                src_ref=stage.at[k],
                dst_ref=gather.at[k, core, me // 2],
                send_sem=send_sem,
                recv_sem=recv_sem.at[k],
                device_id={"ta": to},
            ).start()

        def one(d, carry):
            send(far_first(me, 2 * d), gather_send, gather_recv)
            if k == SWEEPS:
                send(far_first(partner, 2 * d), share_send, share_recv)
            return carry

        lax.fori_loop(1, chips, one, 0)
        if k == SWEEPS:
            send(partner, share_send, share_recv)

    def share_large(k):
        gather_copy(k, pl.ds(0, chips - 1)).wait_recv()
        if k < SWEEPS:
            share_copy(k).start()

    def exchange_small(k, value):
        small_stage[k] = value
        small[k, me] = value

        def one(d, carry):
            pltpu.make_async_remote_copy(
                src_ref=small_stage.at[k],
                dst_ref=small.at[k, me],
                send_sem=small_send,
                recv_sem=small_recv.at[k],
                device_id={"ta": far_first(me, d)},
            ).start()
            return carry

        lax.fori_loop(1, n, one, 0)
        pending.append(
            pltpu.make_async_remote_copy(
                src_ref=small.at[k, pl.ds(0, n - 1)],
                dst_ref=small.at[k, pl.ds(0, n - 1)],
                send_sem=small_send,
                recv_sem=small_recv.at[k],
                device_id={"ta": right},
            )
        )

    def apply_links(s, vectors, first, last):
        k = slice(first * comps, last * comps)
        return fold(dot(vectors, lcat[s, 0, k]) + dot(vectors, lcat[s, 1, k]))

    def across(s):
        return (s + sites // 2) % sites, s ^ 1

    def load_inner(f):
        for s in range(sites):
            parts[s] = stacked_parts(field[f, s * rhs : (s + 1) * rhs])

    def inner(send=None):
        for s in range(sites):
            if send is not None:
                send_site(*send, s)
            y, z = across(s)
            vectors = jnp.concatenate([parts[s], parts[y], parts[z]], axis=1)
            acc[s * rhs : (s + 1) * rhs] = apply_links(s, vectors, 0, INNER_SUMS)

    def outer(r, f, to, of_field, of_links, send=None, keep=False):
        def arrived(rows, s):
            pltpu.make_async_remote_copy(
                src_ref=halo.at[r, :, rows],
                dst_ref=halo.at[r, :, rows],
                send_sem=halo_send,
                recv_sem=halo_arrival(r, s),
                device_id={"ta": left},
            ).wait_recv()

        if r == SWEEPS:
            arrived(slice(None), 0)

        def site(s, carry):
            if r != SWEEPS:
                arrived(rows_of(s), s)
            vectors = jnp.concatenate(
                [stacked_parts(halo[r, side, rows_of(s)]) for side in range(2)], axis=1
            )
            links = acc[rows_of(s)] + apply_links(s, vectors, INNER_SUMS, sums)
            new = of_field * field[f, rows_of(s)] + of_links * links
            field[to, rows_of(s)] = new
            if send is not None:
                send_site(send, to, s)
            if keep:
                parts[s] = stacked_parts(new)
            return carry

        lax.fori_loop(0, sites, site, 0)

    def image_of(c):
        last = len(c) - 1
        inside = [(c[i] - c[i - 1]) / STEP for i in range(1, last + 1)]
        return [c[0] / STEP] + inside + [-c[last] / STEP]

    def factor_of(gram, c, d):
        gd = [
            functools.reduce(jnp.add, [gram(i, j) * d[j] for j in range(len(d))])
            for i in range(len(d))
        ]
        across = functools.reduce(jnp.add, [gd[i] * c[i] for i in range(len(c))])
        squared = functools.reduce(jnp.add, [gd[i] * d[i] for i in range(len(d))])
        return DAMPING * across / squared

    def advance(c, x, d, factor):
        x = [x[i] + factor * c[i] if i < len(c) else x[i] for i in range(SWEEPS)]
        return [c[i] - factor * d[i] if i < len(c) else -factor * d[i] for i in range(len(d))], x

    def sweeps(gram, count):
        c = [jnp.ones((1, width), F32)]
        x = [jnp.zeros((1, width), F32)] * SWEEPS
        for _ in range(count):
            d = image_of(c)
            c, x = advance(c, x, d, factor_of(gram, c, d))
        return c, x

    def combine(coefficients, fields):
        return functools.reduce(jnp.add, [a * field[f] for a, f in zip(coefficients, fields)])

    images[...] = jnp.zeros(images.shape, BF16)
    inputs[0].wait()
    pl.semaphore_wait(barrier, n - 1)
    send_field(0, 0)
    load_inner(0)
    inputs[1].wait()
    prol_copies = near(0, prol_in, prol_halo)
    prol_parts = stacked_parts(prol_in[...])

    def prepare(s, carry):
        pltpu.make_async_copy(links_ref.at[0, s], raw.at[s], link_sem.at[s]).wait()
        for at, members in enumerate(LINK_SUMS):
            hi, lo = two_parts(functools.reduce(jnp.add, [raw[s, m] for m in members]).T)
            lcat[s, 0, at * comps : (at + 1) * comps] = hi
            lcat[s, 1, at * comps : (at + 1) * comps] = lo
        return carry

    lax.fori_loop(0, sites, prepare, 0)
    for k in range(SWEEPS + 1):
        value = jnp.concatenate(
            [restrict(), products([(field[k], field[i]) for i in range(k + 1)])], axis=0
        )
        exchange_large(k, value)
        if k == SWEEPS:
            send_field(k, k)
            for copy in prol_copies:
                copy.start()
        inner()
        if k:
            share_large(k - 1)
        if k < SWEEPS:
            outer(k, k, k + 1, 1.0 - STEP, -STEP, k + 1 if k + 1 < SWEEPS else None, True)

    inputs[2].wait()
    inverse_parts = stacked_parts(inverse_in[...])

    def total_of(slots, k, at, rows):
        return jnp.sum(slots.at[k][:, at : at + rows, :], axis=0)

    def unpack(total, i):
        row = total[i // sites : i // sites + 1]
        return over_sites(jnp.where(lane_site == i % sites, row, 0.0))

    def solve_coarse(coefficients):
        def spread(chip, carry):
            for half_chip in range(2):
                r = functools.reduce(
                    jnp.add,
                    [a * gather[k, half_chip, chip, :ks] for k, a in enumerate(coefficients)],
                )
                for s in range(sites):
                    hi, lo = two_parts(jnp.where(lane_site == s, r, 0.0))
                    row = ((2 * chip + half_chip) * sites + s) * ks
                    at = pl.ds(pl.multiple_of(row, ks), ks)
                    rall[at, :width] = hi
                    rall[at, width:] = lo
            return carry

        lax.fori_loop(0, chips, spread, 0, unroll=4)
        return over_sites(dot_parts(inverse_parts, rall[...]))

    grams = {}

    def gram(i, j):
        return grams[max(i, j), min(i, j)]

    def read_grams(k):
        share_copy(k).wait_recv()
        total = functools.reduce(jnp.add, [total_of(gather, (k, c), ks, 1) for c in range(2)])
        grams.update({(k, i): unpack(total, i) for i in range(k + 1)})

    for k in range(SWEEPS):
        read_grams(k)
    c, x = sweeps(gram, SWEEPS - 1)
    d = image_of(c)
    before = solve_coarse(c)
    share_large(SWEEPS)
    read_grams(SWEEPS)
    factor = factor_of(gram, c, d)
    coarse = before - factor * solve_coarse(d)
    coarse_out[...] = jnp.concatenate([coarse, jnp.zeros((width - half, width), F32)], axis=0).T[:rhs]
    coarse_copies = near(1, coarse_out, coarse_halo)
    for copy in coarse_copies:
        copy.start()
    c, x = advance(c, x, d, factor)
    turned = columns(c + x)
    c, x = turned[: len(c)], turned[len(c) :]
    field[7] = combine(c, range(SWEEPS + 1))

    def both_arrived(k, dst):
        pltpu.make_async_remote_copy(
            src_ref=dst,
            dst_ref=dst,
            send_sem=near_send.at[k],
            recv_sem=near_recv.at[k],
            device_id={"ta": left},
        ).wait_recv()

    both_arrived(0, prol_halo)
    for at, block in enumerate((prol_in, prol_halo.at[0], prol_halo.at[1])):
        for s in range(sites):
            prol_sites[at, s] = stacked_parts(block[s * ks : (s + 1) * ks])
    for s in range(sites):
        y, z = across(s)
        terms = ((0, 0, s), (1, 0, y), (2, 0, z), (3, 1, s), (4, 2, s))
        for m, at, site in terms:
            value = apply_links(s, prol_sites[at, site], m, m + 1)
            if m == 0:
                value = value + prol_in[s * ks : (s + 1) * ks]
            row = at * half + site * ks
            images[s, 0, row : row + ks], images[s, 1, row : row + ks] = two_parts(value)

    def vectors_of(block):
        return stacked_parts(block[:, :half])

    def part_of(s, vectors, at):
        k = slice(at * half, (at + 1) * half)
        return fold(dot(vectors, images[s, 0, k]) + dot(vectors, images[s, 1, k]))

    own = vectors_of(coarse_out[...])
    for s in range(sites):
        acc_coarse[s * rhs : (s + 1) * rhs] = part_of(s, own, 0)
    both_arrived(1, coarse_halo)
    around = jnp.concatenate([vectors_of(coarse_halo[side]) for side in range(2)], axis=1)
    for s in range(sites):
        k = slice(half, 3 * half)
        links = fold(dot(around, images[s, 0, k]) + dot(around, images[s, 1, k]))
        new = acc_coarse[s * rhs : (s + 1) * rhs] + links
        field[6, s * rhs : (s + 1) * rhs] = new
        if s < sites // 2:
            send_site(4, 6, s)
    exchange_small(0, products([(field[6], field[7]), (field[6], field[6])], SMALL_ROWS))
    for s in range(sites // 2, sites):
        send_site(4, 6, s)
    load_inner(6)
    outer(SWEEPS, SWEEPS, SWEEPS + 1, 1.0 - STEP, -STEP)
    inner()
    field[8] = combine(c, range(1, SWEEPS + 2))
    field[9] = combine(x, range(SWEEPS))
    spread_hi, spread_lo = two_parts(jnp.where(diagonal, coarse, 0.0).T)
    field[5] = (
        dot(spread_hi, prol_parts[:half])
        + dot(spread_lo, prol_parts[:half])
        + dot(spread_hi, prol_parts[half:])
    )
    outer(4, 6, 14, 1.0 - STEP, -STEP)
    pending[-1].wait_recv()
    pair = total_of(small, 0, 0, SMALL_ROWS)
    g = columns([unpack(pair, 0) / unpack(pair, 1)])[0]

    for s in range(sites):
        at = slice(s * rhs, (s + 1) * rhs)
        new = field[8, at] - g[at] * field[14, at]
        field[11, at] = new
        parts[s] = stacked_parts(new)
    inner((5, 11))
    field[10] = field[7] - g * field[6]
    field[9] = field[9] + g * field[5]
    outer(5, 11, 12, 1.0 - STEP, -STEP, 6, True)
    early = [(i, j) for i in range(3) for j in range(i + 1)]
    late = [(3, j) for j in range(4)]
    exchange_small(1, products([(field[10 + i], field[10 + j]) for i, j in early], SMALL_ROWS))
    inner()
    outer(6, 12, 13, 1.0 - STEP, -STEP)
    exchange_small(2, products([(field[10 + i], field[10 + j]) for i, j in late], SMALL_ROWS))
    def all_sent(ref, sem):
        pltpu.make_async_remote_copy(
            src_ref=ref, dst_ref=ref, send_sem=sem, recv_sem=late_recv, device_id={"ta": left}
        ).wait_send()

    all_sent(halo, halo_send)
    all_sent(gather.at[:, 0, pl.ds(0, chips - 1)], gather_send)
    all_sent(gather.at[:, 0], share_send)
    all_sent(prol_halo, near_send.at[0])
    all_sent(coarse_halo, near_send.at[1])
    pending[-2].wait_recv()
    total = total_of(small, 1, 0, SMALL_ROWS)
    grams = {pair: unpack(total, early.index(pair)) for pair in early}
    c, x = sweeps(gram, SWEEPS - 1)
    d = image_of(c)
    pending[-1].wait_recv()
    total = total_of(small, 2, 0, SMALL_ROWS)
    grams.update({pair: unpack(total, late.index(pair)) for pair in late})
    c, x = advance(c, x, d, factor_of(gram, c, d))
    turned = columns(c + x)
    residual_ref[...] = combine(turned[: len(c)], range(10, 14))
    solution_ref[...] = field[9] + combine(turned[len(c) :], range(10, 13))
    all_sent(small.at[:, pl.ds(0, n - 1)], small_send)


def hand_over(*refs):
    copies = [pltpu.make_async_copy(refs[i], refs[2 + i], refs[4].at[i]) for i in range(2)]
    for copy in copies:
        copy.start()
    for copy in copies:
        copy.wait()


def local(source, links, prolongator, coarse_inverse):
    n = lax.axis_size("ta")
    shape = source.shape
    _, sites, rhs, comps = shape
    ks = prolongator.shape[2]
    width, half = sites * rhs, sites * ks
    sums = len(LINK_SUMS)
    vmem = pl.BlockSpec(memory_space=pltpu.VMEM)
    dma = pltpu.SemaphoreType.DMA
    fields = (jax.ShapeDtypeStruct((width, comps), F32),) * 2
    results = pl.pallas_call(
        functools.partial(kernel, n),
        out_shape=(pltpu.VMEM((width, comps), F32),) * 2,
        in_specs=[pl.BlockSpec(memory_space=pl.ANY)] * 4,
        out_specs=(vmem, vmem),
        scratch_shapes=[
            pltpu.VMEM((half, comps), F32),
            pltpu.VMEM(coarse_inverse.shape, F32),
            pltpu.VMEM(links.shape[1:], F32),
            pltpu.VMEM((sites, 2, sums * comps, comps), BF16),
            pltpu.VMEM((15, width, comps), F32),
            pltpu.VMEM((sites, 2 * rhs, comps), BF16),
            pltpu.VMEM((width, comps), F32),
            pltpu.VMEM((7, 2, width, comps), F32),
            pltpu.VMEM((2, half, comps), F32),
            pltpu.VMEM((3, sites, 2 * ks, comps), BF16),
            pltpu.VMEM((sites, 2, 4 * half, comps), BF16),
            pltpu.VMEM((rhs, width), F32),
            pltpu.VMEM((2, rhs, width), F32),
            pltpu.VMEM((width, comps), F32),
            pltpu.VMEM((SWEEPS + 1, ks + 1, width), F32),
            pltpu.VMEM((SWEEPS + 1, 2, n // 2, ks + 1, width), F32),
            pltpu.VMEM((3, SMALL_ROWS, width), F32),
            pltpu.VMEM((3, n, SMALL_ROWS, width), F32),
            pltpu.VMEM((n * half, 2 * width), BF16),
            dma((3,)),
            dma((sites,)),
            dma,
            dma((2, sites)),
            dma,
            dma((2,)),
            dma((2,)),
            dma,
            dma((SWEEPS + 1,)),
            dma,
            dma((SWEEPS + 1,)),
            dma,
            dma((3,)),
        ],
        compiler_params=pltpu.CompilerParams(
            collective_id=0, has_side_effects=True, vmem_limit_bytes=60 * 1024 * 1024
        ),
    )(
        source.reshape(width, comps),
        links,
        prolongator.reshape(half, comps),
        coarse_inverse,
    )
    results = pl.pallas_call(
        hand_over, out_shape=fields, in_specs=[vmem] * 2,
        out_specs=(pl.BlockSpec(memory_space=pl.ANY),) * 2, scratch_shapes=[dma((2,))],
        compiler_params=pltpu.CompilerParams(vmem_limit_bytes=1024 * 1024),
    )(*[pltpu.with_memory_space_constraint(r, pltpu.VMEM) for r in results])
    return tuple(r.reshape(shape) for r in results)


def solution(mesh):
    return jax.shard_map(
        local,
        mesh=mesh,
        in_specs=(
            P(("groups", "ta"), None, None, None),
            P("ta", None, None, None, None),
            P("ta", None, None, None),
            P("ta", None),
        ),
        out_specs=(P(("groups", "ta"), None, None, None), P(("groups", "ta"), None, None, None)),
        check_vma=False,
    )
```
